256 devices in a mesh: dp: 8 (over x, y_hi), seq: 32 (over y_lo, z, core).
Axes of the slice: x: 4, y: 4 (y_hi: 2, y_lo: 2; y = y_hi * 2 + y_lo), z: 8, core: 2. Of those that a mesh axis runs over, the one named last changes fastest.
Arguments:
- inputs: bfloat16 [8, 16384, 1024], P('dp', 'seq'), may hold values from -6 to 6
- out_grad: bfloat16 [8, 16384, 1024], P('dp', 'seq'), may hold values from -6 to 6
- w_in: bfloat16 [1024, 3072], replicated, may hold values from -0.1875 to 0.1875
- taps: float32 [3, 3072], replicated, may hold values from -3 to 3
- filt: bfloat16 [64, 256, 1024], P(None, 'seq'), may hold values from -4 to 4
Outputs:
- mixed: bfloat16 [8, 16384, 1024], P('dp', 'seq')
- in_grad: bfloat16 [8, 16384, 1024], P('dp', 'seq')
- w_in_grad: float32 [1024, 3072], P('dp', 'seq')
- taps_grad: float32 [3, 3072], replicated
The draws below stay inside these ranges and needn't reach their ends.
All inputs are finite; a program needn't handle non-finite values.
Results may differ from the reference program's by a relative error of at most 0.012.
Values may be sent and summed in bfloat16 or wider, within the bound.
A program may use at most 128 MiB of HBM per device.

```python
import math
import jax
import jax.numpy as jnp
from jax import lax

D = 1024
BLK = 256
LENGTH = 16384
SEQS = 8
SPAN = 64


def draw_taps(key, part):
    normal = jax.random.normal(key, (3, 3 * D), jnp.float32)
    spread = jnp.array([1.0, 0.3, 1.0], jnp.float32)[:, None]
    return jnp.clip(normal * spread, -3.0, 3.0)


def block_levels(rng, shape, split, smallest, high):
    def one(dim, blocks):
        draws = jax.random.uniform(jax.random.fold_in(jax.random.fold_in(rng, 6), dim), (blocks,), jnp.float32, smallest / len(split), high / len(split))
        return jnp.repeat(jnp.exp(draws), shape[dim] // blocks).reshape((-1,) + (1,) * (len(shape) - dim - 1))

    factor_of = one(*split[0])
    for cut in split[1:]:
        factor_of = factor_of * one(*cut)
    return factor_of


def scatter_about(own_key, dims, deviation, most, shards=(), held_as=jnp.bfloat16):
    values = deviation * jax.random.normal(own_key, dims, jnp.float32)
    if shards:
        values = values * block_levels(own_key, dims, shards, -0.22, 0.18)
    return jnp.clip(values, -most, most).astype(held_as)


def setup_inputs(seed: int = 0) -> dict:
    key_of = jax.random.split(jax.random.key(seed), 6)
    inputs = scatter_about(key_of[0], (SEQS, LENGTH, D), 1.0, 6.0, ((0, 8), (1, 32)))
    out_grad = scatter_about(key_of[1], (SEQS, LENGTH, D), 1.0, 6.0, ((0, 8), (1, 32)))
    w_in = scatter_about(key_of[2], (D, 3 * D), D ** -0.5, 0.1875)
    taps = draw_taps(jax.random.fold_in(key_of[5], 71), 0)
    filt = scatter_about(key_of[4], (SPAN, BLK, D), 1.0, 4.0, ((1, 32),))
    return dict(inputs=inputs, out_grad=out_grad, w_in=w_in, taps=taps, filt=filt)


def dct_table(count):
    rows = jnp.arange(count, dtype=jnp.float32)[:, None]
    cols = jnp.arange(count, dtype=jnp.float32)[None, :]
    first = jnp.where(rows == 0, jnp.float32(math.sqrt(0.5)), jnp.float32(1.0))
    table = jnp.float32(math.sqrt(2.0 / count)) * first * jnp.cos(jnp.float32(math.pi) * (cols + 0.5) * rows / count)
    return table.astype(jnp.bfloat16)

def monarch(source, filt, table_q, table_p):
    hi = lax.Precision.HIGHEST
    blocks = source.reshape(SPAN, BLK, D).astype(jnp.float32)
    tq = table_q.astype(jnp.float32)
    tp = table_p.astype(jnp.float32)
    first = jnp.einsum('rq,pqd->prd', tq, blocks, precision=hi).astype(jnp.bfloat16)
    second = jnp.einsum('ap,prd->ard', tp, first.astype(jnp.float32), precision=hi)
    scaled = (filt.astype(jnp.float32) * second).astype(jnp.bfloat16)
    third = jnp.einsum('ap,ard->prd', tp, scaled.astype(jnp.float32), precision=hi).astype(jnp.bfloat16)
    last = jnp.einsum('rq,prd->pqd', tq, third.astype(jnp.float32), precision=hi)
    return last.reshape(LENGTH, D)

def reference(inputs, out_grad, w_in, taps, filt):
    table_q = dct_table(BLK)
    table_p = dct_table(SPAN)
    factor = 1.0 / math.sqrt(SEQS * LENGTH)

    def one(carry, pair):
        rows, grads = pair
        z = jnp.dot(rows, w_in, preferred_element_type=jnp.float32).astype(jnp.bfloat16)
        zpad = jnp.pad(z, ((1, 1), (0, 0)))
        s = taps[0] * zpad[:-2] + taps[1] * zpad[1:-1] + taps[2] * zpad[2:]
        a_part = s[:, :D]
        g_part = s[:, D:2 * D]
        v_part = s[:, 2 * D:]
        w = (a_part * v_part).astype(jnp.bfloat16)
        gradf = grads.astype(jnp.float32)
        e4 = (gradf * g_part).astype(jnp.bfloat16)
        h4 = monarch(w, filt, table_q, table_p)
        dw = monarch(e4, filt, table_q, table_p)
        mixed = (g_part * h4).astype(jnp.bfloat16)
        ds = jnp.concatenate([dw * v_part, gradf * h4, dw * a_part], axis=1).astype(jnp.bfloat16)
        dspad = jnp.pad(ds, ((1, 1), (0, 0)))
        du = (taps[0] * dspad[2:] + taps[1] * dspad[1:-1] + taps[2] * dspad[:-2]).astype(jnp.bfloat16)
        in_grad = jnp.dot(du, w_in.T, preferred_element_type=jnp.float32).astype(jnp.bfloat16)
        wgrad = jnp.dot(rows.T, du, preferred_element_type=jnp.float32)
        dsf = ds.astype(jnp.float32)
        zf = zpad.astype(jnp.float32)
        tgrad = jnp.stack([lax.optimization_barrier(jnp.sum(dsf * zf[k:k + LENGTH], axis=0)) for k in range(3)])
        return ((carry[0] + wgrad, carry[1] + tgrad), (mixed, in_grad))
    init = (jnp.zeros((D, 3 * D), jnp.float32), jnp.zeros((3, 3 * D), jnp.float32))
    (wgrad, tgrad), (mixed, in_grad) = lax.scan(one, init, (inputs, out_grad))
    return (mixed, in_grad, wgrad * factor, tgrad * factor)
```

```python
import functools
import math

import jax
import jax.numpy as jnp
import numpy as np
from jax import lax
from jax.experimental import pallas as pl
from jax.experimental.pallas import tpu as pltpu
from jax.sharding import PartitionSpec as P

BLK = 256
NC = 4
RT = 64
MESH = pl.DeviceIdType.MESH
F32 = jnp.float32
BF16 = jnp.bfloat16


def dct_table(count):
    rows = np.arange(count, dtype=np.float32)[:, None]
    cols = np.arange(count, dtype=np.float32)[None, :]
    first = np.where(rows == 0, np.float32(math.sqrt(0.5)), np.float32(1.0))
    angle = np.float32(math.pi) * (cols + np.float32(0.5)) * rows / np.float32(count)
    table = np.float32(math.sqrt(2.0 / count)) * first * np.cos(angle.astype(np.float32))
    return table.astype(np.float32)


def tables(nseq, nb):
    share = BLK // nseq
    span = nb * nseq
    size = nb * BLK
    cq = dct_table(BLK)
    cp = dct_table(span)
    first = np.zeros((nseq, nb, share, nb, BLK), np.float32)
    for b in range(nb):
        first[:, b, :, b, :] = cq.reshape(nseq, share, BLK)
    first = first.reshape(size, size)
    second = np.zeros((span, share, span, share), np.float32)
    for r in range(share):
        second[:, r, :, r] = cp
    second = second.reshape(size, size)
    return np.stack([first, second, first.T, second.T]).astype(jnp.bfloat16)


def kernel(
    n,
    x_hbm,
    og_hbm,
    w_hbm,
    taps,
    filt_hbm,
    tab_hbm,
    mixed_hbm,
    ing_hbm,
    wg_hbm,
    tg,
    xv,
    ogv,
    wv,
    fv,
    tab,
    zb,
    sb,
    ub,
    s1,
    r1,
    s2,
    r2,
    hd,
    dsb,
    dub,
    acc,
    mx,
    igb,
    wgb,
    xsem,
    tabsem,
    wsem,
    ogsem,
    fsem,
    hs_sem,
    hr_sem,
    ss1,
    rs1,
    ss2,
    rs2,
    ds_s,
    ds_r,
    mxsem,
    igsem,
    wgsem,
):
    tok, width = x_hbm.shape
    cw = width // NC
    rows2 = r1.shape[2]
    me = lax.axis_index("seq")
    right, left = lax.rem(me + 1, n), lax.rem(me + n - 1, n)

    def cols(g, k):
        return pl.ds(pl.multiple_of(g * width + k * cw, cw), cw)

    xcopy = pltpu.make_async_copy(x_hbm, xv.at[pl.ds(0, tok)], xsem)
    xcopy.start()

    def wcopy(k, g):
        return pltpu.make_async_copy(w_hbm.at[:, cols(g, k)], wv.at[k * 3 + g], wsem.at[k * 3 + g])

    def ogcopy(k):
        return pltpu.make_async_copy(og_hbm.at[:, cols(0, k)], ogv.at[k], ogsem.at[k])

    def fcopy(k):
        return pltpu.make_async_copy(filt_hbm.at[:, cols(0, k)], fv.at[k], fsem.at[k])

    tabcopy = pltpu.make_async_copy(tab_hbm, tab, tabsem)
    for g in range(3):
        wcopy(0, g).start()
    ogcopy(0).start()
    tabcopy.start()

    @pl.loop(1, NC)
    def _(k):
        for g in range(3):
            wcopy(k, g).start()
        ogcopy(k).start()

    @pl.loop(0, NC)
    def _(k):
        fcopy(k).start()

    barrier = pltpu.get_barrier_semaphore()

    @pl.loop(1, n)
    def _(d):
        pl.semaphore_signal(
            barrier, inc=1, device_id={"seq": lax.rem(me + d, n)}, device_id_type=MESH
        )

    xcopy.wait()
    pl.semaphore_wait(barrier, n - 1)

    def xhalo(side):
        src = xv.at[pl.ds(tok - 16, 16)] if side == 0 else xv.at[pl.ds(0, 16)]
        dst = xv.at[pl.ds(tok, 16)] if side == 0 else xv.at[pl.ds(tok + 16, 16)]
        return pltpu.make_async_remote_copy(
            src_ref=src,
            dst_ref=dst,
            send_sem=hs_sem.at[side],
            recv_sem=hr_sem.at[side],
            device_id={"seq": right if side == 0 else left},
            device_id_type=MESH,
        )

    xhalo(0).start()
    xhalo(1).start()
    xhalo(0).wait()
    xhalo(1).wait()
    tabcopy.wait()
    lmask = jnp.where(me == 0, 0.0, 1.0).astype(F32)
    rmask = jnp.where(me == n - 1, 0.0, 1.0).astype(F32)

    def spread(src, dst, ssem, rsem, k):
        @pl.loop(1, n)
        def _(d):
            peer = lax.rem(me + d, n)
            pltpu.make_async_remote_copy(
                src_ref=src.at[k, peer],
                dst_ref=dst.at[k, me],
                send_sem=ssem.at[k],
                recv_sem=rsem.at[k],
                device_id={"seq": peer},
                device_id_type=MESH,
            ).start()

        pltpu.make_async_copy(src.at[k, me], dst.at[k, me], rsem.at[k]).start()

    def arrived(dst, rsem, k):
        pltpu.make_async_copy(dst.at[k], dst.at[k], rsem.at[k]).wait()

    def sent(src, ssem, k):
        part = src.at[k, pl.ds(0, n - 1)]
        pltpu.make_async_copy(part, part, ssem.at[k]).wait()

    def shifted(blk):
        size = RT + 16
        prev = pltpu.roll(blk, 1, 0)[8 : 8 + RT]
        nxt = pltpu.roll(blk, size - 1, 0)[8 : 8 + RT]
        return prev, blk[8 : 8 + RT], nxt

    def stage1(k):
        for g in range(3):
            wcopy(k, g).wait()
            kk = k * 3 + g
            z = jnp.dot(xv[...], wv[kk], preferred_element_type=F32).astype(BF16).astype(F32)
            zb[kk, pl.ds(8, tok), :] = z[:tok]
            zb[kk, pl.ds(0, 8), :] = z[tok + 8 : tok + 16] * lmask
            zb[kk, pl.ds(8 + tok, 8), :] = z[tok + 16 : tok + 24] * rmask
        ogcopy(k).wait()

        @pl.loop(0, tok // RT)
        def _(i):
            base = pl.multiple_of(i * RT, RT)
            parts = []
            for g in range(3):
                kk = k * 3 + g
                prev, here, nxt = shifted(zb[kk, pl.ds(base, RT + 16), :])
                t = taps[:, cols(g, k)]
                s = t[0:1] * prev + t[1:2] * here + t[2:3] * nxt
                sb[kk, pl.ds(base, RT), :] = s
                parts.append(s)
            a, gate, v = parts
            grad = ogv[k, pl.ds(base, RT), :].astype(F32)
            ub[pl.ds(base, RT), pl.ds(0, cw)] = (a * v).astype(BF16)
            ub[pl.ds(base, RT), pl.ds(cw, cw)] = (grad * gate).astype(BF16)

        for h in range(2):
            hc = pl.ds(h * cw, cw)
            h1 = jnp.dot(tab[0], ub[:, hc], preferred_element_type=F32).astype(BF16)
            s1[k, :, :, hc] = h1.reshape(n, rows2, cw)
        spread(s1, r1, ss1, rs1, k)

    def stage2(k):
        arrived(r1, rs1, k)
        fcopy(k).wait()
        for h in range(2):
            hc = pl.ds(h * cw, cw)
            got = r1[k, :, :, hc].reshape(tok, cw)
            h2 = jnp.dot(tab[1], got, preferred_element_type=F32)
            f = (fv[k].astype(F32) * h2).astype(BF16)
            h3 = jnp.dot(tab[3], f, preferred_element_type=F32).astype(BF16)
            s2[k, :, :, hc] = h3.reshape(n, rows2, cw)
        spread(s2, r2, ss2, rs2, k)

    def dshalo(k, side):
        group = pl.ds(k * 3, 3)
        if side == 0:
            src, dst = dsb.at[group, pl.ds(tok, 8)], dsb.at[group, pl.ds(0, 8)]
        else:
            src, dst = dsb.at[group, pl.ds(8, 8)], dsb.at[group, pl.ds(8 + tok, 8)]
        return pltpu.make_async_remote_copy(
            src_ref=src,
            dst_ref=dst,
            send_sem=ds_s.at[k, side],
            recv_sem=ds_r.at[k, side],
            device_id={"seq": right if side == 0 else left},
            device_id_type=MESH,
        )

    def mxcopy(k):
        return pltpu.make_async_copy(mx.at[k], mixed_hbm.at[:, cols(0, k)], mxsem.at[k])

    def stage3(k):
        arrived(r2, rs2, k)
        for h in range(2):
            got = r2[k, :, :, pl.ds(h * cw, cw)].reshape(tok, cw)
            hd[h] = jnp.dot(tab[2], got, preferred_element_type=F32)

        @pl.loop(0, tok // RT)
        def _(i):
            base = pl.multiple_of(i * RT, RT)
            at = pl.ds(base, RT)
            h4, dw = hd[0, at, :], hd[1, at, :]
            a, gate, v = (sb[k * 3 + g, at, :] for g in range(3))
            grad = ogv[k, at, :].astype(F32)
            mx[k, at, :] = (gate * h4).astype(BF16)
            inner = pl.ds(base + 8, RT)
            dsb[k * 3, inner, :] = (dw * v).astype(BF16).astype(F32)
            dsb[k * 3 + 1, inner, :] = (grad * h4).astype(BF16).astype(F32)
            dsb[k * 3 + 2, inner, :] = (dw * a).astype(BF16).astype(F32)

        dshalo(k, 0).start()
        dshalo(k, 1).start()
        mxcopy(k).start()

    def stage4(k):
        dshalo(k, 0).wait()
        dshalo(k, 1).wait()

        @pl.when(me == 0)
        def _():
            dsb[pl.ds(k * 3, 3), pl.ds(0, 8), :] = jnp.zeros((3, 8, cw), F32)

        @pl.when(me == n - 1)
        def _():
            dsb[pl.ds(k * 3, 3), pl.ds(8 + tok, 8), :] = jnp.zeros((3, 8, cw), F32)

        def rows(i, sums):
            base = pl.multiple_of(i * RT, RT)
            out = []
            for g in range(3):
                kk = k * 3 + g
                prev, here, nxt = shifted(dsb[kk, pl.ds(base, RT + 16), :])
                t = taps[:, cols(g, k)]
                du = t[0:1] * nxt + t[1:2] * here + t[2:3] * prev
                dub[g, pl.ds(base, RT), :] = du.astype(BF16)
                for j, z in enumerate(shifted(zb[kk, pl.ds(base, RT + 16), :])):
                    out.append(
                        sums[g * 3 + j] + jnp.sum((here * z).reshape(RT // 8, 8, cw), axis=0)
                    )
            return tuple(out)

        sums = lax.fori_loop(0, tok // RT, rows, tuple(jnp.zeros((8, cw), F32) for _ in range(9)))
        for g in range(3):
            tg[:, cols(g, k)] = jnp.concatenate(
                [jnp.sum(sums[g * 3 + j], axis=0, keepdims=True) for j in range(3)], axis=0
            )

        nt = (((1,), (1,)), ((), ()))
        tn = (((0,), (0,)), ((), ()))

        @pl.loop(0, width // 256)
        def _(j):
            at = pl.ds(pl.multiple_of(j * 256, 256), 256)
            total = jnp.zeros((tok, 256), F32)
            for g in range(3):
                total += lax.dot_general(
                    dub[g], wv[k * 3 + g, at, :], nt, preferred_element_type=F32
                )

            @pl.when(k == 0)
            def _():
                acc[j] = total

            @pl.when(k > 0)
            def _():
                acc[j] += total

            for g in range(3):
                wgb[k * 3 + g, at, :] = lax.dot_general(
                    xv[pl.ds(0, tok), at], dub[g], tn, preferred_element_type=F32
                ).astype(BF16)

        for g in range(3):
            wgcopy(k, g).start()

    def wgcopy(k, g):
        return pltpu.make_async_copy(
            wgb.at[k * 3 + g], wg_hbm.at[:, cols(g, k)], wgsem.at[k * 3 + g]
        )

    @pl.loop(0, NC)
    def _(k):
        stage1(k)

    @pl.loop(0, NC + 2)
    def _(t):
        @pl.when(t < NC)
        def _():
            stage2(t)

        @pl.when((t >= 1) & (t <= NC))
        def _():
            stage3(t - 1)

        @pl.when(t >= 2)
        def _():
            stage4(t - 2)

    igs = []
    for j in range(width // 256):
        at = pl.ds(j * 256, 256)
        igb[:, at] = acc[j].astype(BF16)
        copy = pltpu.make_async_copy(igb.at[:, at], ing_hbm.at[:, at], igsem.at[j])
        copy.start()
        igs.append(copy)

    @pl.loop(0, NC)
    def _(k):
        sent(s1, ss1, k)
        sent(s2, ss2, k)
        mxcopy(k).wait()
        for g in range(3):
            wgcopy(k, g).wait()

    for copy in igs:
        copy.wait()


def fused(rows, grads, w_in, taps, filt, n):
    tok, width = rows.shape
    nb = tok // BLK
    cw = width // NC
    share = BLK // n
    tab = jnp.asarray(tables(n, nb))
    any_space = pl.BlockSpec(memory_space=pl.ANY)
    vmem = pl.BlockSpec(memory_space=pltpu.VMEM)
    dma = pltpu.SemaphoreType.DMA
    return pl.pallas_call(
        functools.partial(kernel, n),
        out_shape=(
            jax.ShapeDtypeStruct((tok, width), BF16),
            jax.ShapeDtypeStruct((tok, width), BF16),
            jax.ShapeDtypeStruct((width, 3 * width), BF16),
            jax.ShapeDtypeStruct((3, 3 * width), F32),
        ),
        in_specs=[any_space, any_space, any_space, vmem, any_space, any_space],
        out_specs=(any_space, any_space, any_space, vmem),
        scratch_shapes=[
            pltpu.VMEM((tok + 32, width), BF16),
            pltpu.VMEM((NC, tok, cw), BF16),
            pltpu.VMEM((3 * NC, width, cw), BF16),
            pltpu.VMEM((NC, tok, cw), BF16),
            pltpu.VMEM((4, tok, tok), BF16),
            pltpu.VMEM((3 * NC, tok + 16, cw), F32),
            pltpu.VMEM((3 * NC, tok, cw), F32),
            pltpu.VMEM((tok, 2 * cw), BF16),
            pltpu.VMEM((NC, n, nb * share, 2 * cw), BF16),
            pltpu.VMEM((NC, n, nb * share, 2 * cw), BF16),
            pltpu.VMEM((NC, n, nb * share, 2 * cw), BF16),
            pltpu.VMEM((NC, n, nb * share, 2 * cw), BF16),
            pltpu.VMEM((2, tok, cw), F32),
            pltpu.VMEM((3 * NC, tok + 16, cw), F32),
            pltpu.VMEM((3, tok, cw), BF16),
            pltpu.VMEM((width // 256, tok, 256), F32),
            pltpu.VMEM((NC, tok, cw), BF16),
            pltpu.VMEM((tok, width), BF16),
            pltpu.VMEM((3 * NC, width, cw), BF16),
            dma,
            dma,
            dma((3 * NC,)),
            dma((NC,)),
            dma((NC,)),
            dma((2,)),
            dma((2,)),
            dma((NC,)),
            dma((NC,)),
            dma((NC,)),
            dma((NC,)),
            dma((NC, 2)),
            dma((NC, 2)),
            dma((NC,)),
            dma((width // 256,)),
            dma((3 * NC,)),
        ],
        compiler_params=pltpu.CompilerParams(
            collective_id=0, has_side_effects=True, vmem_limit_bytes=67043328
        ),
        name="monarch",
    )(rows, grads, w_in, taps, filt.reshape(tok, width), tab)


def shards(inputs, out_grad, w_in, taps, filt):
    tok = inputs.shape[1]
    nseq = lax.axis_size("seq")
    ndata = lax.axis_size("dp")
    factor = 1.0 / math.sqrt(ndata * nseq * tok)
    mixed, in_grad, wg, local_taps = fused(inputs[0], out_grad[0], w_in, taps, filt, nseq)
    taps_grad = lax.psum(local_taps, ("dp", "seq")) * factor
    partial_sum = lax.psum_scatter(wg, "dp", scatter_dimension=0, tiled=True)
    w_grad = lax.psum_scatter(partial_sum, "seq", scatter_dimension=1, tiled=True)
    return (mixed[None], in_grad[None], w_grad.astype(F32) * factor, taps_grad)


def solution(mesh):
    return jax.shard_map(
        shards,
        mesh=mesh,
        in_specs=(P("dp", "seq", None), P("dp", "seq", None), P(), P(), P(None, "seq", None)),
        out_specs=(P("dp", "seq", None), P("dp", "seq", None), P("dp", "seq"), P()),
        check_vma=False,
    )
```

```python
import functools
import math

import jax
import jax.numpy as jnp
import numpy as np
from jax import lax
from jax.experimental import pallas as pl
from jax.experimental.pallas import tpu as pltpu
from jax.sharding import PartitionSpec as P

BLK = 256
NC = 4
RT = 64
MESH = pl.DeviceIdType.MESH
F32 = jnp.float32
BF16 = jnp.bfloat16


def dct_table(count):
    rows = np.arange(count, dtype=np.float32)[:, None]
    cols = np.arange(count, dtype=np.float32)[None, :]
    first = np.where(rows == 0, np.float32(math.sqrt(0.5)), np.float32(1.0))
    angle = np.float32(math.pi) * (cols + np.float32(0.5)) * rows / np.float32(count)
    table = np.float32(math.sqrt(2.0 / count)) * first * np.cos(angle.astype(np.float32))
    return table.astype(np.float32)


def tables(nseq, nb):
    share = BLK // nseq
    span = nb * nseq
    size = nb * BLK
    cq = dct_table(BLK)
    cp = dct_table(span)
    first = np.zeros((nseq, nb, share, nb, BLK), np.float32)
    for b in range(nb):
        first[:, b, :, b, :] = cq.reshape(nseq, share, BLK)
    first = first.reshape(size, size)
    second = np.zeros((span, share, span, share), np.float32)
    for r in range(share):
        second[:, r, :, r] = cp
    second = second.reshape(size, size)
    return np.stack([first, second, first.T, second.T]).astype(jnp.bfloat16)


def kernel(
    n,
    ndp,
    factor,
    x_hbm,
    og_hbm,
    w_hbm,
    taps,
    filt_hbm,
    tab_hbm,
    mixed_hbm,
    ing_hbm,
    wg_out,
    tg_out,
    xv,
    ogv,
    wv,
    fv,
    tab,
    zb,
    sb,
    ub,
    s1,
    r1,
    s2,
    r2,
    hd,
    dsb,
    dub,
    acc,
    xt,
    wgb,
    cr,
    xr,
    ys,
    yr,
    fs,
    fr,
    tb,
    tr,
    t2s,
    t2r,
    t3r,
    xsem,
    tabsem,
    wsem,
    ogsem,
    fsem,
    hs_sem,
    hr_sem,
    ss1,
    rs1,
    ss2,
    rs2,
    ds_s,
    ds_r,
    mxsem,
    igsem,
    c_s,
    c_r,
    x_s,
    x_r,
    y_s,
    y_r,
    f_s,
    f_r,
    t_s,
    t_r,
):
    tok, width = x_hbm.shape
    cw = width // NC
    rows2 = r1.shape[2]
    me = lax.axis_index("seq")
    right, left = lax.rem(me + 1, n), lax.rem(me + n - 1, n)
    dpi = lax.axis_index("dp")
    xn = ndp // 2
    xi, yh = dpi // 2, lax.rem(dpi, 2)
    core = lax.rem(me, 2)
    sibling = me + 1 - 2 * core

    def cols(g, k):
        return pl.ds(pl.multiple_of(g * width + k * cw, cw), cw)

    xcopy = pltpu.make_async_copy(x_hbm, xv.at[pl.ds(0, tok)], xsem)
    xcopy.start()

    def wcopy(k, g):
        return pltpu.make_async_copy(w_hbm.at[:, cols(g, k)], wv.at[k * 3 + g], wsem.at[k * 3 + g])

    def ogcopy(k):
        return pltpu.make_async_copy(og_hbm.at[:, cols(0, k)], ogv.at[k], ogsem.at[k])

    def fcopy(k):
        return pltpu.make_async_copy(filt_hbm.at[:, cols(0, k)], fv.at[k], fsem.at[k])

    tabcopy = pltpu.make_async_copy(tab_hbm, tab, tabsem)
    for g in range(3):
        wcopy(0, g).start()
    ogcopy(0).start()
    tabcopy.start()

    @pl.loop(1, NC)
    def _(k):
        for g in range(3):
            wcopy(k, g).start()
        ogcopy(k).start()

    @pl.loop(0, NC)
    def _(k):
        fcopy(k).start()

    barrier = pltpu.get_barrier_semaphore()

    @pl.loop(1, n)
    def _(d):
        pl.semaphore_signal(
            barrier, inc=1, device_id={"seq": lax.rem(me + d, n)}, device_id_type=MESH
        )

    @pl.loop(1, ndp)
    def _(d):
        pl.semaphore_signal(
            barrier, inc=1, device_id={"dp": lax.rem(dpi + d, ndp)}, device_id_type=MESH
        )

    xcopy.wait()
    for c in range(2):
        for q in range(xn):
            xt[c, pl.ds(q * 128, 128), :] = xv[pl.ds(0, tok), pl.ds((2 * q + c) * 128, 128)].T
    pl.semaphore_wait(barrier, n + ndp - 2)

    def xhalo(side):
        src = xv.at[pl.ds(tok - 16, 16)] if side == 0 else xv.at[pl.ds(0, 16)]
        dst = xv.at[pl.ds(tok, 16)] if side == 0 else xv.at[pl.ds(tok + 16, 16)]
        return pltpu.make_async_remote_copy(
            src_ref=src,
            dst_ref=dst,
            send_sem=hs_sem.at[side],
            recv_sem=hr_sem.at[side],
            device_id={"seq": right if side == 0 else left},
            device_id_type=MESH,
        )

    xhalo(0).start()
    xhalo(1).start()
    xhalo(0).wait()
    xhalo(1).wait()
    tabcopy.wait()
    lmask = jnp.where(me == 0, 0.0, 1.0).astype(F32)
    rmask = jnp.where(me == n - 1, 0.0, 1.0).astype(F32)

    def spread(src, dst, ssem, rsem, k):
        @pl.loop(1, n)
        def _(d):
            peer = lax.rem(me + d, n)
            pltpu.make_async_remote_copy(
                src_ref=src.at[k, peer],
                dst_ref=dst.at[k, me],
                send_sem=ssem.at[k],
                recv_sem=rsem.at[k],
                device_id={"seq": peer},
                device_id_type=MESH,
            ).start()

        pltpu.make_async_copy(src.at[k, me], dst.at[k, me], rsem.at[k]).start()

    def arrived(dst, rsem, k):
        pltpu.make_async_copy(dst.at[k], dst.at[k], rsem.at[k]).wait()

    def sent(src, ssem, k):
        part = src.at[k, pl.ds(0, n - 1)]
        pltpu.make_async_copy(part, part, ssem.at[k]).wait()

    def shifted(blk):
        size = RT + 16
        prev = pltpu.roll(blk, 1, 0)[8 : 8 + RT]
        nxt = pltpu.roll(blk, size - 1, 0)[8 : 8 + RT]
        return prev, blk[8 : 8 + RT], nxt

    def stage1(k):
        for g in range(3):
            wcopy(k, g).wait()
            kk = k * 3 + g
            z = jnp.dot(xv[...], wv[kk], preferred_element_type=F32).astype(BF16).astype(F32)
            zb[kk, pl.ds(8, tok), :] = z[:tok]
            zb[kk, pl.ds(0, 8), :] = z[tok + 8 : tok + 16] * lmask
            zb[kk, pl.ds(8 + tok, 8), :] = z[tok + 16 : tok + 24] * rmask
        ogcopy(k).wait()

        @pl.loop(0, tok // RT)
        def _(i):
            base = pl.multiple_of(i * RT, RT)
            parts = []
            for g in range(3):
                kk = k * 3 + g
                prev, here, nxt = shifted(zb[kk, pl.ds(base, RT + 16), :])
                t = taps[:, cols(g, k)]
                s = t[0:1] * prev + t[1:2] * here + t[2:3] * nxt
                sb[kk, pl.ds(base, RT), :] = s
                parts.append(s)
            a, gate, v = parts
            grad = ogv[k, pl.ds(base, RT), :].astype(F32)
            ub[pl.ds(base, RT), pl.ds(0, cw)] = (a * v).astype(BF16)
            ub[pl.ds(base, RT), pl.ds(cw, cw)] = (grad * gate).astype(BF16)

        for h in range(2):
            hc = pl.ds(h * cw, cw)
            h1 = jnp.dot(tab[0], ub[:, hc], preferred_element_type=F32).astype(BF16)
            s1[k, :, :, hc] = h1.reshape(n, rows2, cw)
        spread(s1, r1, ss1, rs1, k)

    def stage2(k):
        arrived(r1, rs1, k)
        fcopy(k).wait()
        for h in range(2):
            hc = pl.ds(h * cw, cw)
            got = r1[k, :, :, hc].reshape(tok, cw)
            h2 = jnp.dot(tab[1], got, preferred_element_type=F32)
            f = (fv[k].astype(F32) * h2).astype(BF16)
            h3 = jnp.dot(tab[3], f, preferred_element_type=F32).astype(BF16)
            s2[k, :, :, hc] = h3.reshape(n, rows2, cw)
        spread(s2, r2, ss2, rs2, k)

    def dshalo(k, side):
        group = pl.ds(k * 3, 3)
        if side == 0:
            src, dst = dsb.at[group, pl.ds(tok, 8)], dsb.at[group, pl.ds(0, 8)]
        else:
            src, dst = dsb.at[group, pl.ds(8, 8)], dsb.at[group, pl.ds(8 + tok, 8)]
        return pltpu.make_async_remote_copy(
            src_ref=src,
            dst_ref=dst,
            send_sem=ds_s.at[k, side],
            recv_sem=ds_r.at[k, side],
            device_id={"seq": right if side == 0 else left},
            device_id_type=MESH,
        )

    def mxcopy(k):
        return pltpu.make_async_copy(ogv.at[k], mixed_hbm.at[:, cols(0, k)], mxsem.at[k])

    def stage3(k):
        arrived(r2, rs2, k)
        for h in range(2):
            got = r2[k, :, :, pl.ds(h * cw, cw)].reshape(tok, cw)
            hd[h] = jnp.dot(tab[2], got, preferred_element_type=F32)

        @pl.loop(0, tok // RT)
        def _(i):
            base = pl.multiple_of(i * RT, RT)
            at = pl.ds(base, RT)
            h4, dw = hd[0, at, :], hd[1, at, :]
            a, gate, v = (sb[k * 3 + g, at, :] for g in range(3))
            grad = ogv[k, at, :].astype(F32)
            ogv[k, at, :] = (gate * h4).astype(BF16)
            inner = pl.ds(base + 8, RT)
            dsb[k * 3, inner, :] = (dw * v).astype(BF16).astype(F32)
            dsb[k * 3 + 1, inner, :] = (grad * h4).astype(BF16).astype(F32)
            dsb[k * 3 + 2, inner, :] = (dw * a).astype(BF16).astype(F32)

        dshalo(k, 0).start()
        dshalo(k, 1).start()
        mxcopy(k).start()

    def stage4(k):
        dshalo(k, 0).wait()
        dshalo(k, 1).wait()

        @pl.when(me == 0)
        def _():
            dsb[pl.ds(k * 3, 3), pl.ds(0, 8), :] = jnp.zeros((3, 8, cw), F32)

        @pl.when(me == n - 1)
        def _():
            dsb[pl.ds(k * 3, 3), pl.ds(8 + tok, 8), :] = jnp.zeros((3, 8, cw), F32)

        def rows(i, sums):
            base = pl.multiple_of(i * RT, RT)
            out = []
            for g in range(3):
                kk = k * 3 + g
                prev, here, nxt = shifted(dsb[kk, pl.ds(base, RT + 16), :])
                t = taps[:, cols(g, k)]
                du = t[0:1] * nxt + t[1:2] * here + t[2:3] * prev
                dub[g, pl.ds(base, RT), :] = du.astype(BF16)
                for j, z in enumerate(shifted(zb[kk, pl.ds(base, RT + 16), :])):
                    out.append(
                        sums[g * 3 + j] + jnp.sum((here * z).reshape(RT // 8, 8, cw), axis=0)
                    )
            return tuple(out)

        sums = lax.fori_loop(0, tok // RT, rows, tuple(jnp.zeros((8, cw), F32) for _ in range(9)))
        sums = [jnp.sum(part, axis=0, keepdims=True) for part in sums]
        packed = jnp.concatenate(sums + [jnp.zeros((7, cw), F32)], axis=0)
        for q in range(cw // 128):
            tb[k * (cw // 128) + q] = packed[:, q * 128 : (q + 1) * 128]

        for g in range(3):
            wgb[k * 3 + g, 1 - core] = jnp.dot(
                xt[1 - core], dub[g], preferred_element_type=F32
            ).astype(BF16)
        ccopy(k).start()

        nt = (((1,), (1,)), ((), ()))

        @pl.loop(0, width // 256)
        def _(j):
            at = pl.ds(pl.multiple_of(j * 256, 256), 256)
            total = jnp.zeros((tok, 256), F32)
            for g in range(3):
                total += lax.dot_general(
                    dub[g], wv[k * 3 + g, at, :], nt, preferred_element_type=F32
                )

            @pl.when(k == 0)
            def _():
                acc[j] = total

            @pl.when(k > 0)
            def _():
                acc[j] += total

        ccopy(k).wait_recv()
        for g in range(3):
            own = jnp.dot(xt[core], dub[g], preferred_element_type=F32)
            wgb[k * 3 + g, core] = (own + cr[k * 3 + g].astype(F32)).astype(BF16)
        for d in range(1, xn):
            xcopy_out(k, lax.rem(xi + d, xn)).start()

    def ccopy(k):
        group = pl.ds(k * 3, 3)
        return pltpu.make_async_remote_copy(
            src_ref=wgb.at[group, 1 - core],
            dst_ref=cr.at[group],
            send_sem=c_s.at[k],
            recv_sem=c_r.at[k],
            device_id={"seq": sibling},
            device_id_type=MESH,
        )

    def block(q):
        return pl.ds(pl.multiple_of(q * 128, 128), 128)

    def xcopy_out(k, q):
        return pltpu.make_async_remote_copy(
            src_ref=wgb.at[pl.ds(k * 3, 3), core, block(q)],
            dst_ref=xr.at[k, xi],
            send_sem=x_s.at[k],
            recv_sem=x_r.at[k],
            device_id={"dp": q * 2 + yh},
            device_id_type=MESH,
        )

    def ycopy(k):
        return pltpu.make_async_remote_copy(
            src_ref=ys.at[k],
            dst_ref=yr.at[k],
            send_sem=y_s.at[k],
            recv_sem=y_r.at[k],
            device_id={"dp": xi * 2 + 1 - yh},
            device_id_type=MESH,
        )

    def local_wait(ref, sem):
        pltpu.make_async_copy(ref, ref, sem).wait()

    def stage5(k):
        local_wait(xr.at[k, pl.ds(0, xn - 1)], x_r.at[k])
        for g in range(3):
            total = wgb[k * 3 + g, core, block(xi), :].astype(F32)
            for d in range(1, xn):
                total += xr[k, lax.rem(xi + d, xn), g].astype(F32)
            ys[k, g] = total.astype(BF16)

        @pl.when(yh != core)
        def _():
            ycopy(k).start()

    def stage6(k):
        @pl.when(yh == core)
        def _():
            ycopy(k).wait_recv()
            for g in range(3):
                total = ys[k, g].astype(F32) + yr[k, g].astype(F32)
                fs[pl.ds((k * 3 + g) * (cw // 32), cw // 32)] = (
                    total.T.astype(BF16).reshape(cw // 32, 32, 128)
                )
            for g in range(3):

                @pl.loop(0, cw // 32)
                def _(i):
                    piece = (g * width + k * cw) // 32 + i
                    owner, slot = piece // per, lax.rem(piece, per)
                    src = fs.at[(k * 3 + g) * (cw // 32) + i]
                    dst = fr.at[me // 2, slot]

                    @pl.when(owner == me)
                    def _():
                        pltpu.make_async_copy(src, dst, f_r).start()

                    @pl.when(owner != me)
                    def _():
                        pltpu.make_async_remote_copy(
                            src_ref=src,
                            dst_ref=dst,
                            send_sem=f_s,
                            recv_sem=f_r,
                            device_id={"seq": owner},
                            device_id_type=MESH,
                        ).start()

    per = fr.shape[1]

    def taps_copy(step, src, dst, axis, peer):
        return pltpu.make_async_remote_copy(
            src_ref=src,
            dst_ref=dst,
            send_sem=t_s.at[step],
            recv_sem=t_r.at[step],
            device_id={axis: peer},
            device_id_type=MESH,
        )

    @pl.loop(0, NC)
    def _(k):
        stage1(k)

    @pl.loop(0, NC + 2)
    def _(t):
        @pl.when(t < NC)
        def _():
            stage2(t)

        @pl.when((t >= 1) & (t <= NC))
        def _():
            stage3(t - 1)

        @pl.when(t >= 2)
        def _():
            stage4(t - 2)

        @pl.when(t >= 3)
        def _():
            stage5(t - 3)

        @pl.when(t >= 4)
        def _():
            stage6(t - 4)

    tr[dpi] = tb[dpi]

    @pl.loop(1, ndp)
    def _(d):
        peer = lax.rem(dpi + d, ndp)
        taps_copy(0, tb.at[peer], tr.at[dpi], "dp", peer).start()

    igs = []
    for j in range(NC):
        fv[j] = acc[j].astype(BF16)
        copy = pltpu.make_async_copy(
            fv.at[j], ing_hbm.at[:, pl.ds(j * cw, cw)], igsem.at[j]
        )
        copy.start()
        igs.append(copy)

    stage6(NC - 2)
    stage5(NC - 1)

    local_wait(tr.at[pl.ds(0, ndp - 1)], t_r.at[0])
    total = tr[0]
    for m in range(1, ndp):
        total += tr[m]
    t2s[...] = total

    @pl.loop(1, n)
    def _(d):
        peer = lax.rem(me + d, n)
        taps_copy(1, t2s, t2r.at[me], "seq", peer).start()

    pltpu.make_async_copy(t2s, t2r.at[me], t_r.at[1]).start()
    stage6(NC - 1)

    local_wait(t2r, t_r.at[1])
    t3r[dpi] = lax.fori_loop(0, n, lambda i, c: c + t2r[i], jnp.zeros((16, 128), F32)) * factor

    @pl.loop(1, ndp)
    def _(d):
        taps_copy(2, t3r.at[dpi], t3r.at[dpi], "dp", lax.rem(dpi + d, ndp)).start()

    local_wait(fr, f_r)
    for p in range(per):
        wg_out[pl.ds(p * 32, 32), :] = (
            lax.fori_loop(
                0, n // 2, lambda i, c, p=p: c + fr[i, p].astype(F32), jnp.zeros((32, 128), F32)
            )
            * factor
        )

    local_wait(t3r.at[pl.ds(0, ndp - 1)], t_r.at[2])
    for m in range(ndp):
        for g in range(3):
            tg_out[:, pl.ds(g * width + m * 128, 128)] = t3r[m, pl.ds(g * 3, 3), :]

    @pl.loop(0, NC)
    def _(k):
        sent(s1, ss1, k)
        sent(s2, ss2, k)
        mxcopy(k).wait()
        ccopy(k).wait_send()
        local_wait(xr.at[k, pl.ds(0, xn - 1)], x_s.at[k])

        @pl.when(yh != core)
        def _():
            ycopy(k).wait_send()

    @pl.when(yh == core)
    def _():
        local_wait(fs.at[pl.ds(0, fs.shape[0] - per)], f_s)

    local_wait(tr.at[pl.ds(0, ndp - 1)], t_s.at[0])
    local_wait(t2r.at[pl.ds(0, n - 1)], t_s.at[1])
    local_wait(tr.at[pl.ds(0, ndp - 1)], t_s.at[2])
    for copy in igs:
        copy.wait()


def fused(rows, grads, w_in, taps, filt, n, ndp, factor):
    tok, width = rows.shape
    nb = tok // BLK
    cw = width // NC
    share = BLK // n
    per = 3 * width // n // 32
    assert cw == 256 and width == 128 * ndp and ndp % 2 == 0 and per * 32 * n == 3 * width
    tab = jnp.asarray(tables(n, nb))
    any_space = pl.BlockSpec(memory_space=pl.ANY)
    vmem = pl.BlockSpec(memory_space=pltpu.VMEM)
    dma = pltpu.SemaphoreType.DMA
    return pl.pallas_call(
        functools.partial(kernel, n, ndp, factor),
        out_shape=(
            jax.ShapeDtypeStruct((tok, width), BF16),
            jax.ShapeDtypeStruct((tok, width), BF16),
            jax.ShapeDtypeStruct((per * 32, 128), F32),
            jax.ShapeDtypeStruct((3, 3 * width), F32),
        ),
        in_specs=[any_space, any_space, any_space, vmem, any_space, any_space],
        out_specs=(any_space, any_space, vmem, vmem),
        scratch_shapes=[
            pltpu.VMEM((tok + 32, width), BF16),
            pltpu.VMEM((NC, tok, cw), BF16),
            pltpu.VMEM((3 * NC, width, cw), BF16),
            pltpu.VMEM((NC, tok, cw), BF16),
            pltpu.VMEM((4, tok, tok), BF16),
            pltpu.VMEM((3 * NC, tok + 16, cw), F32),
            pltpu.VMEM((3 * NC, tok, cw), F32),
            pltpu.VMEM((tok, 2 * cw), BF16),
            pltpu.VMEM((NC, n, nb * share, 2 * cw), BF16),
            pltpu.VMEM((NC, n, nb * share, 2 * cw), BF16),
            pltpu.VMEM((NC, n, nb * share, 2 * cw), BF16),
            pltpu.VMEM((NC, n, nb * share, 2 * cw), BF16),
            pltpu.VMEM((2, tok, cw), F32),
            pltpu.VMEM((3 * NC, tok + 16, cw), F32),
            pltpu.VMEM((3, tok, cw), BF16),
            pltpu.VMEM((width // 256, tok, 256), F32),
            pltpu.VMEM((2, 64 * ndp, tok), BF16),
            pltpu.VMEM((3 * NC, 2, 64 * ndp, cw), BF16),
            pltpu.VMEM((3 * NC, 64 * ndp, cw), BF16),
            pltpu.VMEM((NC, ndp // 2, 3, 128, cw), BF16),
            pltpu.VMEM((NC, 3, 128, cw), BF16),
            pltpu.VMEM((NC, 3, 128, cw), BF16),
            pltpu.VMEM((per * n, 32, 128), BF16),
            pltpu.VMEM((n // 2, per, 32, 128), BF16),
            pltpu.VMEM((ndp, 16, 128), F32),
            pltpu.VMEM((ndp, 16, 128), F32),
            pltpu.VMEM((16, 128), F32),
            pltpu.VMEM((n, 16, 128), F32),
            pltpu.VMEM((ndp, 16, 128), F32),
            dma,
            dma,
            dma((3 * NC,)),
            dma((NC,)),
            dma((NC,)),
            dma((2,)),
            dma((2,)),
            dma((NC,)),
            dma((NC,)),
            dma((NC,)),
            dma((NC,)),
            dma((NC, 2)),
            dma((NC, 2)),
            dma((NC,)),
            dma((NC,)),
            dma((NC,)),
            dma((NC,)),
            dma((NC,)),
            dma((NC,)),
            dma((NC,)),
            dma((NC,)),
            dma,
            dma,
            dma((3,)),
            dma((3,)),
        ],
        compiler_params=pltpu.CompilerParams(
            collective_id=0, has_side_effects=True, vmem_limit_bytes=67043328
        ),
        name="monarch",
    )(rows, grads, w_in, taps, filt.reshape(tok, width), tab)


def shards(inputs, out_grad, w_in, taps, filt):
    tok = inputs.shape[1]
    nseq = lax.axis_size("seq")
    ndata = lax.axis_size("dp")
    factor = 1.0 / math.sqrt(ndata * nseq * tok)
    mixed, in_grad, w_grad, taps_grad = fused(
        inputs[0], out_grad[0], w_in, taps, filt, nseq, ndata, factor
    )
    return (mixed[None], in_grad[None], w_grad.T, taps_grad)


def solution(mesh):
    return jax.shard_map(
        shards,
        mesh=mesh,
        in_specs=(P("dp", "seq", None), P("dp", "seq", None), P(), P(), P(None, "seq", None)),
        out_specs=(P("dp", "seq", None), P("dp", "seq", None), P("dp", "seq"), P()),
        check_vma=False,
    )
```

```python
import functools
import math

import jax
import jax.numpy as jnp
import numpy as np
from jax import lax
from jax.experimental import pallas as pl
from jax.experimental.pallas import tpu as pltpu
from jax.sharding import PartitionSpec as P

BLK = 256
NC = 4
RT = 64
MESH = pl.DeviceIdType.MESH
F32 = jnp.float32
BF16 = jnp.bfloat16


def dct_table(count):
    rows = np.arange(count, dtype=np.float32)[:, None]
    cols = np.arange(count, dtype=np.float32)[None, :]
    first = np.where(rows == 0, np.float32(math.sqrt(0.5)), np.float32(1.0))
    angle = np.float32(math.pi) * (cols + np.float32(0.5)) * rows / np.float32(count)
    table = np.float32(math.sqrt(2.0 / count)) * first * np.cos(angle.astype(np.float32))
    return table.astype(np.float32)


def tables(nseq, nb):
    share = BLK // nseq
    span = nb * nseq
    size = nb * BLK
    cq = dct_table(BLK)
    cp = dct_table(span)
    first = np.zeros((nseq, nb, share, nb, BLK), np.float32)
    for b in range(nb):
        first[:, b, :, b, :] = cq.reshape(nseq, share, BLK)
    first = first.reshape(size, size)
    second = np.zeros((span, share, span, share), np.float32)
    for r in range(share):
        second[:, r, :, r] = cp
    second = second.reshape(size, size)
    return np.stack([first, second, first.T, second.T]).astype(jnp.bfloat16)


def kernel(
    n,
    ndp,
    factor,
    x_hbm,
    og_hbm,
    w_hbm,
    taps,
    filt_hbm,
    tab_hbm,
    mixed_hbm,
    ing_hbm,
    wg_out,
    tg_out,
    xv,
    ogv,
    wv,
    fv,
    tab,
    zb,
    sb,
    ub,
    s1,
    r1,
    s2,
    r2,
    hd,
    dsb,
    dub,
    acc,
    xt,
    wgb,
    cr,
    xr,
    ys,
    yr,
    fs,
    fr,
    tb,
    tr,
    t2s,
    t2r,
    t3r,
    xsem,
    tabsem,
    wsem,
    ogsem,
    fsem,
    hs_sem,
    hr_sem,
    ss1,
    rs1,
    ss2,
    rs2,
    ds_s,
    ds_r,
    mxsem,
    igsem,
    c_s,
    c_r,
    x_s,
    x_r,
    y_s,
    y_r,
    f_s,
    f_r,
    t_s,
    t_r,
):
    tok, width = x_hbm.shape
    cw = width // NC
    rows2 = r1.shape[2]
    me = lax.axis_index("seq")
    right, left = lax.rem(me + 1, n), lax.rem(me + n - 1, n)
    dpi = lax.axis_index("dp")
    xn = ndp // 2
    xi, yh = dpi // 2, lax.rem(dpi, 2)
    core = lax.rem(me, 2)
    sibling = me + 1 - 2 * core

    def cols(g, k):
        return pl.ds(pl.multiple_of(g * width + k * cw, cw), cw)

    xcopy = pltpu.make_async_copy(x_hbm, xv.at[pl.ds(0, tok)], xsem)
    xcopy.start()

    def wcopy(k, g):
        return pltpu.make_async_copy(w_hbm.at[:, cols(g, k)], wv.at[k * 3 + g], wsem.at[k * 3 + g])

    def ogcopy(k):
        return pltpu.make_async_copy(og_hbm.at[:, cols(0, k)], ogv.at[k], ogsem.at[k])

    def fcopy(k):
        return pltpu.make_async_copy(filt_hbm.at[:, cols(0, k)], fv.at[k], fsem.at[k])

    tabcopy = pltpu.make_async_copy(tab_hbm, tab, tabsem)
    for g in range(3):
        wcopy(0, g).start()
    ogcopy(0).start()
    tabcopy.start()

    @pl.loop(1, NC)
    def _(k):
        for g in range(3):
            wcopy(k, g).start()
        ogcopy(k).start()

    @pl.loop(0, NC)
    def _(k):
        fcopy(k).start()

    barrier = pltpu.get_barrier_semaphore()

    @pl.loop(1, n)
    def _(d):
        pl.semaphore_signal(
            barrier, inc=1, device_id={"seq": lax.rem(me + d, n)}, device_id_type=MESH
        )

    @pl.loop(1, ndp)
    def _(d):
        pl.semaphore_signal(
            barrier, inc=1, device_id={"dp": lax.rem(dpi + d, ndp)}, device_id_type=MESH
        )

    xcopy.wait()
    for c in range(2):
        for q in range(xn):
            xt[c, pl.ds(q * 128, 128), :] = xv[pl.ds(0, tok), pl.ds((2 * q + c) * 128, 128)].T
    pl.semaphore_wait(barrier, n + ndp - 2)

    def xhalo(side):
        src = xv.at[pl.ds(tok - 16, 16)] if side == 0 else xv.at[pl.ds(0, 16)]
        dst = xv.at[pl.ds(tok, 16)] if side == 0 else xv.at[pl.ds(tok + 16, 16)]
        return pltpu.make_async_remote_copy(
            src_ref=src,
            dst_ref=dst,
            send_sem=hs_sem.at[side],
            recv_sem=hr_sem.at[side],
            device_id={"seq": right if side == 0 else left},
            device_id_type=MESH,
        )

    xhalo(0).start()
    xhalo(1).start()
    lmask = jnp.where(me == 0, 0.0, 1.0).astype(F32)
    rmask = jnp.where(me == n - 1, 0.0, 1.0).astype(F32)

    def spread(src, dst, ssem, rsem, k):
        @pl.loop(1, n)
        def _(d):
            peer = lax.rem(me + d, n)
            pltpu.make_async_remote_copy(
                src_ref=src.at[k, peer],
                dst_ref=dst.at[k, me],
                send_sem=ssem.at[k],
                recv_sem=rsem.at[k],
                device_id={"seq": peer},
                device_id_type=MESH,
            ).start()

        pltpu.make_async_copy(src.at[k, me], dst.at[k, me], rsem.at[k]).start()

    def arrived(dst, rsem, k):
        pltpu.make_async_copy(dst.at[k], dst.at[k], rsem.at[k]).wait()

    def sent(src, ssem, k):
        part = src.at[k, pl.ds(0, n - 1)]
        pltpu.make_async_copy(part, part, ssem.at[k]).wait()

    def shifted(blk):
        size = RT + 16
        prev = pltpu.roll(blk, 1, 0)[8 : 8 + RT]
        nxt = pltpu.roll(blk, size - 1, 0)[8 : 8 + RT]
        return prev, blk[8 : 8 + RT], nxt

    def stage1(k):
        for g in range(3):
            wcopy(k, g).wait()
            kk = k * 3 + g
            z = jnp.dot(xv[pl.ds(0, tok)], wv[kk], preferred_element_type=F32)
            zb[kk, pl.ds(8, tok), :] = z.astype(BF16).astype(F32)

        @pl.when(k == 0)
        def _():
            xhalo(0).wait()
            xhalo(1).wait()
            tabcopy.wait()

        for g in range(3):
            kk = k * 3 + g
            z = jnp.dot(xv[pl.ds(tok, 32)], wv[kk], preferred_element_type=F32)
            z = z.astype(BF16).astype(F32)
            zb[kk, pl.ds(0, 8), :] = z[8:16] * lmask
            zb[kk, pl.ds(8 + tok, 8), :] = z[16:24] * rmask
        ogcopy(k).wait()

        @pl.loop(0, tok // RT)
        def _(i):
            base = pl.multiple_of(i * RT, RT)
            parts = []
            for g in range(3):
                kk = k * 3 + g
                prev, here, nxt = shifted(zb[kk, pl.ds(base, RT + 16), :])
                t = taps[:, cols(g, k)]
                s = t[0:1] * prev + t[1:2] * here + t[2:3] * nxt
                sb[kk, pl.ds(base, RT), :] = s
                parts.append(s)
            a, gate, v = parts
            grad = ogv[k, pl.ds(base, RT), :].astype(F32)
            ub[pl.ds(base, RT), pl.ds(0, cw)] = (a * v).astype(BF16)
            ub[pl.ds(base, RT), pl.ds(cw, cw)] = (grad * gate).astype(BF16)

        for h in range(2):
            hc = pl.ds(h * cw, cw)
            h1 = jnp.dot(tab[0], ub[:, hc], preferred_element_type=F32).astype(BF16)
            s1[k, :, :, hc] = h1.reshape(n, rows2, cw)
        spread(s1, r1, ss1, rs1, k)

    def stage2(k):
        arrived(r1, rs1, k)
        fcopy(k).wait()
        for h in range(2):
            hc = pl.ds(h * cw, cw)
            got = r1[k, :, :, hc].reshape(tok, cw)
            h2 = jnp.dot(tab[1], got, preferred_element_type=F32)
            f = (fv[k].astype(F32) * h2).astype(BF16)
            h3 = jnp.dot(tab[3], f, preferred_element_type=F32).astype(BF16)
            s2[k, :, :, hc] = h3.reshape(n, rows2, cw)
        spread(s2, r2, ss2, rs2, k)

    def dshalo(k, side):
        group = pl.ds(k * 3, 3)
        if side == 0:
            src, dst = dsb.at[group, pl.ds(tok, 8)], dsb.at[group, pl.ds(0, 8)]
        else:
            src, dst = dsb.at[group, pl.ds(8, 8)], dsb.at[group, pl.ds(8 + tok, 8)]
        return pltpu.make_async_remote_copy(
            src_ref=src,
            dst_ref=dst,
            send_sem=ds_s.at[k, side],
            recv_sem=ds_r.at[k, side],
            device_id={"seq": right if side == 0 else left},
            device_id_type=MESH,
        )

    def mxcopy(k):
        return pltpu.make_async_copy(ogv.at[k], mixed_hbm.at[:, cols(0, k)], mxsem.at[k])

    def stage3(k):
        arrived(r2, rs2, k)
        for h in range(2):
            got = r2[k, :, :, pl.ds(h * cw, cw)].reshape(tok, cw)
            hd[h] = jnp.dot(tab[2], got, preferred_element_type=F32)

        @pl.loop(0, tok // RT)
        def _(i):
            base = pl.multiple_of(i * RT, RT)
            at = pl.ds(base, RT)
            h4, dw = hd[0, at, :], hd[1, at, :]
            a, gate, v = (sb[k * 3 + g, at, :] for g in range(3))
            grad = ogv[k, at, :].astype(F32)
            ogv[k, at, :] = (gate * h4).astype(BF16)
            inner = pl.ds(base + 8, RT)
            dsb[k * 3, inner, :] = (dw * v).astype(BF16).astype(F32)
            dsb[k * 3 + 1, inner, :] = (grad * h4).astype(BF16).astype(F32)
            dsb[k * 3 + 2, inner, :] = (dw * a).astype(BF16).astype(F32)

        dshalo(k, 0).start()
        dshalo(k, 1).start()
        mxcopy(k).start()

    def stage4(k):
        dshalo(k, 0).wait()
        dshalo(k, 1).wait()

        @pl.when(me == 0)
        def _():
            dsb[pl.ds(k * 3, 3), pl.ds(0, 8), :] = jnp.zeros((3, 8, cw), F32)

        @pl.when(me == n - 1)
        def _():
            dsb[pl.ds(k * 3, 3), pl.ds(8 + tok, 8), :] = jnp.zeros((3, 8, cw), F32)

        def rows(i, sums):
            base = pl.multiple_of(i * RT, RT)
            out = []
            for g in range(3):
                kk = k * 3 + g
                prev, here, nxt = shifted(dsb[kk, pl.ds(base, RT + 16), :])
                t = taps[:, cols(g, k)]
                du = t[0:1] * nxt + t[1:2] * here + t[2:3] * prev
                dub[g, pl.ds(base, RT), :] = du.astype(BF16)
                for j, z in enumerate(shifted(zb[kk, pl.ds(base, RT + 16), :])):
                    out.append(
                        sums[g * 3 + j] + jnp.sum((here * z).reshape(RT // 8, 8, cw), axis=0)
                    )
            return tuple(out)

        sums = lax.fori_loop(0, tok // RT, rows, tuple(jnp.zeros((8, cw), F32) for _ in range(9)))
        sums = [jnp.sum(part, axis=0, keepdims=True) for part in sums]
        packed = jnp.concatenate(sums + [jnp.zeros((7, cw), F32)], axis=0)
        for q in range(cw // 128):
            tb[k * (cw // 128) + q] = packed[:, q * 128 : (q + 1) * 128]

        @pl.when(k == NC - 1)
        def _():
            tr[dpi] = tb[dpi]

            @pl.loop(1, ndp)
            def _(d):
                peer = lax.rem(dpi + d, ndp)
                taps_copy(0, tb.at[peer], tr.at[dpi], "dp", peer).start()

        for g in range(3):
            wgb[k * 3 + g, 1 - core] = jnp.dot(
                xt[1 - core], dub[g], preferred_element_type=F32
            ).astype(BF16)
        ccopy(k).start()

        half = pl.ds(0, 64 * ndp)
        for g in range(3):
            zb[k * 3 + g, half, :] = jnp.dot(xt[core], dub[g], preferred_element_type=F32)
        ccopy(k).wait_recv()
        for g in range(3):
            kk = k * 3 + g
            wgb[kk, core] = (zb[kk, half, :] + cr[kk].astype(F32)).astype(BF16)
        for d in range(1, xn):
            xcopy_out(k, lax.rem(xi + d, xn)).start()

        nt = (((1,), (1,)), ((), ()))

        @pl.loop(0, width // 256)
        def _(j):
            at = pl.ds(pl.multiple_of(j * 256, 256), 256)
            total = jnp.zeros((tok, 256), F32)
            for g in range(3):
                total += lax.dot_general(
                    dub[g], wv[k * 3 + g, at, :], nt, preferred_element_type=F32
                )

            @pl.when(k == 0)
            def _():
                acc[j] = total

            @pl.when(k > 0)
            def _():
                acc[j] += total

    def ccopy(k):
        group = pl.ds(k * 3, 3)
        return pltpu.make_async_remote_copy(
            src_ref=wgb.at[group, 1 - core],
            dst_ref=cr.at[group],
            send_sem=c_s.at[k],
            recv_sem=c_r.at[k],
            device_id={"seq": sibling},
            device_id_type=MESH,
        )

    def block(q):
        return pl.ds(pl.multiple_of(q * 128, 128), 128)

    def xcopy_out(k, q):
        return pltpu.make_async_remote_copy(
            src_ref=wgb.at[pl.ds(k * 3, 3), core, block(q)],
            dst_ref=xr.at[k, xi],
            send_sem=x_s.at[k],
            recv_sem=x_r.at[k],
            device_id={"dp": q * 2 + yh},
            device_id_type=MESH,
        )

    def ycopy(k):
        return pltpu.make_async_remote_copy(
            src_ref=ys.at[k],
            dst_ref=yr.at[k],
            send_sem=y_s.at[k],
            recv_sem=y_r.at[k],
            device_id={"dp": xi * 2 + 1 - yh},
            device_id_type=MESH,
        )

    def local_wait(ref, sem):
        pltpu.make_async_copy(ref, ref, sem).wait()

    def stage5(k):
        local_wait(xr.at[k, pl.ds(0, xn - 1)], x_r.at[k])
        for g in range(3):
            total = wgb[k * 3 + g, core, block(xi), :].astype(F32)
            for d in range(1, xn):
                total += xr[k, lax.rem(xi + d, xn), g].astype(F32)
            ys[k, g] = total.astype(BF16)

        @pl.when(yh != core)
        def _():
            ycopy(k).start()

    def stage6(k):
        @pl.when(yh == core)
        def _():
            ycopy(k).wait_recv()
            for g in range(3):
                total = ys[k, g].astype(F32) + yr[k, g].astype(F32)
                fs[pl.ds((k * 3 + g) * (cw // 32), cw // 32)] = (
                    total.T.astype(BF16).reshape(cw // 32, 32, 128)
                )
            for g in range(3):

                @pl.loop(0, cw // 32)
                def _(i):
                    piece = (g * width + k * cw) // 32 + i
                    owner, slot = piece // per, lax.rem(piece, per)
                    src = fs.at[(k * 3 + g) * (cw // 32) + i]
                    dst = fr.at[me // 2, slot]

                    @pl.when(owner == me)
                    def _():
                        pltpu.make_async_copy(src, dst, f_r).start()

                    @pl.when(owner != me)
                    def _():
                        pltpu.make_async_remote_copy(
                            src_ref=src,
                            dst_ref=dst,
                            send_sem=f_s,
                            recv_sem=f_r,
                            device_id={"seq": owner},
                            device_id_type=MESH,
                        ).start()

    per = fr.shape[1]

    def taps_copy(step, src, dst, axis, peer):
        return pltpu.make_async_remote_copy(
            src_ref=src,
            dst_ref=dst,
            send_sem=t_s.at[step],
            recv_sem=t_r.at[step],
            device_id={axis: peer},
            device_id_type=MESH,
        )

    @pl.loop(0, NC)
    def _(k):
        stage1(k)

    @pl.loop(0, NC)
    def _(k):
        stage2(k)

    @pl.loop(0, NC + 1)
    def _(t):
        @pl.when(t >= 2)
        def _():
            stage5(t - 2)

        @pl.when(t >= 3)
        def _():
            stage6(t - 3)

        @pl.when(t >= 1)
        def _():
            stage4(t - 1)

        @pl.when(t < NC)
        def _():
            stage3(t)

    igs = []
    for j in range(NC):
        fv[j] = acc[j].astype(BF16)
        copy = pltpu.make_async_copy(
            fv.at[j], ing_hbm.at[:, pl.ds(j * cw, cw)], igsem.at[j]
        )
        copy.start()
        igs.append(copy)

    stage6(NC - 2)

    local_wait(tr.at[pl.ds(0, ndp - 1)], t_r.at[0])
    total = tr[0]
    for m in range(1, ndp):
        total += tr[m]
    t2s[...] = total

    @pl.loop(1, n)
    def _(d):
        peer = lax.rem(me + d, n)
        taps_copy(1, t2s, t2r.at[me], "seq", peer).start()

    pltpu.make_async_copy(t2s, t2r.at[me], t_r.at[1]).start()
    stage5(NC - 1)

    local_wait(t2r, t_r.at[1])
    t3r[dpi] = lax.fori_loop(0, n, lambda i, c: c + t2r[i], jnp.zeros((16, 128), F32)) * factor

    @pl.loop(1, ndp)
    def _(d):
        taps_copy(2, t3r.at[dpi], t3r.at[dpi], "dp", lax.rem(dpi + d, ndp)).start()

    stage6(NC - 1)

    local_wait(fr, f_r)
    for p in range(per):
        wg_out[pl.ds(p * 32, 32), :] = (
            lax.fori_loop(
                0, n // 2, lambda i, c, p=p: c + fr[i, p].astype(F32), jnp.zeros((32, 128), F32)
            )
            * factor
        )

    local_wait(t3r.at[pl.ds(0, ndp - 1)], t_r.at[2])
    for m in range(ndp):
        for g in range(3):
            tg_out[:, pl.ds(g * width + m * 128, 128)] = t3r[m, pl.ds(g * 3, 3), :]

    @pl.loop(0, NC)
    def _(k):
        sent(s1, ss1, k)
        sent(s2, ss2, k)
        mxcopy(k).wait()
        ccopy(k).wait_send()
        local_wait(xr.at[k, pl.ds(0, xn - 1)], x_s.at[k])

        @pl.when(yh != core)
        def _():
            ycopy(k).wait_send()

    @pl.when(yh == core)
    def _():
        local_wait(fs.at[pl.ds(0, fs.shape[0] - per)], f_s)

    local_wait(tr.at[pl.ds(0, ndp - 1)], t_s.at[0])
    local_wait(t2r.at[pl.ds(0, n - 1)], t_s.at[1])
    local_wait(tr.at[pl.ds(0, ndp - 1)], t_s.at[2])
    for copy in igs:
        copy.wait()


def fused(rows, grads, w_in, taps, filt, n, ndp, factor):
    tok, width = rows.shape
    nb = tok // BLK
    cw = width // NC
    share = BLK // n
    per = 3 * width // n // 32
    assert cw == 256 and width == 128 * ndp and ndp % 2 == 0 and per * 32 * n == 3 * width
    tab = jnp.asarray(tables(n, nb))
    any_space = pl.BlockSpec(memory_space=pl.ANY)
    vmem = pl.BlockSpec(memory_space=pltpu.VMEM)
    dma = pltpu.SemaphoreType.DMA
    return pl.pallas_call(
        functools.partial(kernel, n, ndp, factor),
        out_shape=(
            jax.ShapeDtypeStruct((tok, width), BF16),
            jax.ShapeDtypeStruct((tok, width), BF16),
            jax.ShapeDtypeStruct((per * 32, 128), F32),
            jax.ShapeDtypeStruct((3, 3 * width), F32),
        ),
        in_specs=[any_space, any_space, any_space, vmem, any_space, any_space],
        out_specs=(any_space, any_space, vmem, vmem),
        scratch_shapes=[
            pltpu.VMEM((tok + 32, width), BF16),
            pltpu.VMEM((NC, tok, cw), BF16),
            pltpu.VMEM((3 * NC, width, cw), BF16),
            pltpu.VMEM((NC, tok, cw), BF16),
            pltpu.VMEM((4, tok, tok), BF16),
            pltpu.VMEM((3 * NC, tok + 16, cw), F32),
            pltpu.VMEM((3 * NC, tok, cw), F32),
            pltpu.VMEM((tok, 2 * cw), BF16),
            pltpu.VMEM((NC, n, nb * share, 2 * cw), BF16),
            pltpu.VMEM((NC, n, nb * share, 2 * cw), BF16),
            pltpu.VMEM((NC, n, nb * share, 2 * cw), BF16),
            pltpu.VMEM((NC, n, nb * share, 2 * cw), BF16),
            pltpu.VMEM((2, tok, cw), F32),
            pltpu.VMEM((3 * NC, tok + 16, cw), F32),
            pltpu.VMEM((3, tok, cw), BF16),
            pltpu.VMEM((width // 256, tok, 256), F32),
            pltpu.VMEM((2, 64 * ndp, tok), BF16),
            pltpu.VMEM((3 * NC, 2, 64 * ndp, cw), BF16),
            pltpu.VMEM((3 * NC, 64 * ndp, cw), BF16),
            pltpu.VMEM((NC, ndp // 2, 3, 128, cw), BF16),
            pltpu.VMEM((NC, 3, 128, cw), BF16),
            pltpu.VMEM((NC, 3, 128, cw), BF16),
            pltpu.VMEM((per * n, 32, 128), BF16),
            pltpu.VMEM((n // 2, per, 32, 128), BF16),
            pltpu.VMEM((ndp, 16, 128), F32),
            pltpu.VMEM((ndp, 16, 128), F32),
            pltpu.VMEM((16, 128), F32),
            pltpu.VMEM((n, 16, 128), F32),
            pltpu.VMEM((ndp, 16, 128), F32),
            dma,
            dma,
            dma((3 * NC,)),
            dma((NC,)),
            dma((NC,)),
            dma((2,)),
            dma((2,)),
            dma((NC,)),
            dma((NC,)),
            dma((NC,)),
            dma((NC,)),
            dma((NC, 2)),
            dma((NC, 2)),
            dma((NC,)),
            dma((NC,)),
            dma((NC,)),
            dma((NC,)),
            dma((NC,)),
            dma((NC,)),
            dma((NC,)),
            dma((NC,)),
            dma,
            dma,
            dma((3,)),
            dma((3,)),
        ],
        compiler_params=pltpu.CompilerParams(
            collective_id=0, has_side_effects=True, vmem_limit_bytes=67043328
        ),
        name="monarch",
    )(rows, grads, w_in, taps, filt.reshape(tok, width), tab)


def finish_kernel(mixed, ing, wg, tg, mixed_out, ing_out, wg_out, tg_out, buf, isem, osem):
    parts = isem.shape[1]
    size = mixed.shape[0] // parts

    def move(a, j, src, dst, sem):
        return pltpu.make_async_copy(src, dst, sem.at[a, j])

    def fetch(a, j):
        at = pl.ds(j * size, size)
        return move(a, j, (mixed, ing)[a].at[at], buf.at[a, at], isem)

    def put(a, j):
        at = pl.ds(j * size, size)
        return move(a, j, buf.at[a, at], (mixed_out, ing_out)[a].at[at], osem)

    pieces = [(a, j) for j in range(parts) for a in range(2)]
    for piece in pieces:
        fetch(*piece).start()
    wg_out[...] = wg[...]
    tg_out[...] = tg[...]
    for piece in pieces:
        fetch(*piece).wait()
        put(*piece).start()
    for piece in pieces:
        put(*piece).wait()


def finish(mixed, ing, wg, tg):
    any_space = pl.BlockSpec(memory_space=pl.ANY)
    vmem = pl.BlockSpec(memory_space=pltpu.VMEM)
    dma = pltpu.SemaphoreType.DMA((2, 4))
    return pl.pallas_call(
        finish_kernel,
        out_shape=(
            jax.ShapeDtypeStruct(mixed.shape, mixed.dtype),
            jax.ShapeDtypeStruct(ing.shape, ing.dtype),
            jax.ShapeDtypeStruct(wg.shape, wg.dtype),
            jax.ShapeDtypeStruct(tg.shape, tg.dtype),
        ),
        in_specs=[any_space, any_space, vmem, vmem],
        out_specs=(any_space, any_space, vmem, vmem),
        scratch_shapes=[pltpu.VMEM((2, *mixed.shape), mixed.dtype), dma, dma],
        name="finish",
    )(mixed, ing, wg, tg)


def shards(inputs, out_grad, w_in, taps, filt):
    tok = inputs.shape[1]
    nseq = lax.axis_size("seq")
    ndata = lax.axis_size("dp")
    factor = 1.0 / math.sqrt(ndata * nseq * tok)
    mixed, in_grad, w_grad, taps_grad = fused(
        inputs[0], out_grad[0], w_in, taps, filt, nseq, ndata, factor
    )
    mixed, in_grad, w_grad, taps_grad = finish(mixed, in_grad, w_grad, taps_grad)
    return (mixed[None], in_grad[None], w_grad.T, taps_grad)


def solution(mesh):
    return jax.shard_map(
        shards,
        mesh=mesh,
        in_specs=(P("dp", "seq", None), P("dp", "seq", None), P(), P(), P(None, "seq", None)),
        out_specs=(P("dp", "seq", None), P("dp", "seq", None), P("dp", "seq"), P()),
        check_vma=False,
    )
```

```python
import functools
import math

import jax
import jax.numpy as jnp
import numpy as np
from jax import lax
from jax.experimental import pallas as pl
from jax.experimental.pallas import tpu as pltpu
from jax.sharding import PartitionSpec as P

BLK = 256
NC = 4
RT = 64
MESH = pl.DeviceIdType.MESH
F32 = jnp.float32
BF16 = jnp.bfloat16


def dct_table(count):
    rows = np.arange(count, dtype=np.float32)[:, None]
    cols = np.arange(count, dtype=np.float32)[None, :]
    first = np.where(rows == 0, np.float32(math.sqrt(0.5)), np.float32(1.0))
    angle = np.float32(math.pi) * (cols + np.float32(0.5)) * rows / np.float32(count)
    table = np.float32(math.sqrt(2.0 / count)) * first * np.cos(angle.astype(np.float32))
    return table.astype(np.float32)


def tables(nseq, nb):
    share = BLK // nseq
    span = nb * nseq
    size = nb * BLK
    cq = dct_table(BLK)
    cp = dct_table(span)
    first = np.zeros((nseq, nb, share, nb, BLK), np.float32)
    for b in range(nb):
        first[:, b, :, b, :] = cq.reshape(nseq, share, BLK)
    first = first.reshape(size, size)
    second = np.zeros((span, share, span, share), np.float32)
    for r in range(share):
        second[:, r, :, r] = cp
    second = second.reshape(size, size)
    return np.stack([first, second, first.T, second.T]).astype(jnp.bfloat16)


def kernel(
    n,
    ndp,
    factor,
    x_hbm,
    og_hbm,
    w_hbm,
    taps,
    filt_hbm,
    tab_hbm,
    mixed_hbm,
    ing_hbm,
    wg_out,
    tg_out,
    xv,
    ogv,
    wv,
    fv,
    tab,
    zb,
    sb,
    ub,
    s1,
    r1,
    s2,
    r2,
    hd,
    dsb,
    dub,
    acc,
    xt,
    wgb,
    cr,
    xr,
    ys,
    yr,
    fs,
    fr,
    tb,
    tr,
    t2s,
    t2r,
    t3r,
    xsem,
    tabsem,
    wsem,
    ogsem,
    fsem,
    hs_sem,
    hr_sem,
    ss1,
    rs1,
    ss2,
    rs2,
    ds_s,
    ds_r,
    mxsem,
    igsem,
    c_s,
    c_r,
    x_s,
    x_r,
    y_s,
    y_r,
    f_s,
    f_r,
    t_s,
    t_r,
):
    tok, width = x_hbm.shape
    cw = width // NC
    rows2 = r1.shape[2]
    me = lax.axis_index("seq")
    right, left = lax.rem(me + 1, n), lax.rem(me + n - 1, n)
    dpi = lax.axis_index("dp")
    xn = ndp // 2
    xi, yh = dpi // 2, lax.rem(dpi, 2)
    core = lax.rem(me, 2)
    sibling = me + 1 - 2 * core

    def cols(g, k):
        return pl.ds(pl.multiple_of(g * width + k * cw, cw), cw)

    xcopy = pltpu.make_async_copy(x_hbm, xv.at[pl.ds(0, tok)], xsem)
    xcopy.start()

    def wcopy(k, g):
        return pltpu.make_async_copy(w_hbm.at[:, cols(g, k)], wv.at[k * 3 + g], wsem.at[k * 3 + g])

    def ogcopy(k):
        return pltpu.make_async_copy(og_hbm.at[:, cols(0, k)], ogv.at[k], ogsem.at[k])

    def fcopy(k):
        return pltpu.make_async_copy(filt_hbm.at[:, cols(0, k)], fv.at[k], fsem.at[k])

    tabcopy = pltpu.make_async_copy(tab_hbm, tab, tabsem)
    for g in range(3):
        wcopy(0, g).start()
    ogcopy(0).start()
    tabcopy.start()

    @pl.loop(1, NC)
    def _(k):
        for g in range(3):
            wcopy(k, g).start()
        ogcopy(k).start()

    @pl.loop(0, NC)
    def _(k):
        fcopy(k).start()

    barrier = pltpu.get_barrier_semaphore()

    @pl.loop(1, n)
    def _(d):
        pl.semaphore_signal(
            barrier, inc=1, device_id={"seq": lax.rem(me + d, n)}, device_id_type=MESH
        )

    @pl.loop(1, ndp)
    def _(d):
        pl.semaphore_signal(
            barrier, inc=1, device_id={"dp": lax.rem(dpi + d, ndp)}, device_id_type=MESH
        )

    xcopy.wait()
    for c in range(2):
        for q in range(xn):
            xt[c, pl.ds(q * 128, 128), :] = xv[pl.ds(0, tok), pl.ds((2 * q + c) * 128, 128)].T
    pl.semaphore_wait(barrier, n + ndp - 2)

    def xhalo(side):
        src = xv.at[pl.ds(tok - 16, 16)] if side == 0 else xv.at[pl.ds(0, 16)]
        dst = xv.at[pl.ds(tok, 16)] if side == 0 else xv.at[pl.ds(tok + 16, 16)]
        return pltpu.make_async_remote_copy(
            src_ref=src,
            dst_ref=dst,
            send_sem=hs_sem.at[side],
            recv_sem=hr_sem.at[side],
            device_id={"seq": right if side == 0 else left},
            device_id_type=MESH,
        )

    xhalo(0).start()
    xhalo(1).start()
    xhalo(0).wait()
    xhalo(1).wait()
    tabcopy.wait()
    lmask = jnp.where(me == 0, 0.0, 1.0).astype(F32)
    rmask = jnp.where(me == n - 1, 0.0, 1.0).astype(F32)

    def spread(src, dst, ssem, rsem, k):
        @pl.loop(1, n)
        def _(d):
            peer = lax.rem(me + d, n)
            pltpu.make_async_remote_copy(
                src_ref=src.at[k, peer],
                dst_ref=dst.at[k, me],
                send_sem=ssem.at[k],
                recv_sem=rsem.at[k],
                device_id={"seq": peer},
                device_id_type=MESH,
            ).start()

        pltpu.make_async_copy(src.at[k, me], dst.at[k, me], rsem.at[k]).start()

    def arrived(dst, rsem, k):
        pltpu.make_async_copy(dst.at[k], dst.at[k], rsem.at[k]).wait()

    def sent(src, ssem, k):
        part = src.at[k, pl.ds(0, n - 1)]
        pltpu.make_async_copy(part, part, ssem.at[k]).wait()

    def shifted(blk):
        size = RT + 16
        prev = pltpu.roll(blk, 1, 0)[8 : 8 + RT]
        nxt = pltpu.roll(blk, size - 1, 0)[8 : 8 + RT]
        return prev, blk[8 : 8 + RT], nxt

    def stage1(k):
        for g in range(3):
            wcopy(k, g).wait()
            kk = k * 3 + g
            z = jnp.dot(xv[...], wv[kk], preferred_element_type=F32).astype(BF16).astype(F32)
            zb[kk, pl.ds(8, tok), :] = z[:tok]
            zb[kk, pl.ds(0, 8), :] = z[tok + 8 : tok + 16] * lmask
            zb[kk, pl.ds(8 + tok, 8), :] = z[tok + 16 : tok + 24] * rmask
        ogcopy(k).wait()

        @pl.loop(0, tok // RT)
        def _(i):
            base = pl.multiple_of(i * RT, RT)
            parts = []
            for g in range(3):
                kk = k * 3 + g
                prev, here, nxt = shifted(zb[kk, pl.ds(base, RT + 16), :])
                t = taps[:, cols(g, k)]
                s = t[0:1] * prev + t[1:2] * here + t[2:3] * nxt
                sb[kk, pl.ds(base, RT), :] = s
                parts.append(s)
            a, gate, v = parts
            grad = ogv[k, pl.ds(base, RT), :].astype(F32)
            ub[pl.ds(base, RT), pl.ds(0, cw)] = (a * v).astype(BF16)
            ub[pl.ds(base, RT), pl.ds(cw, cw)] = (grad * gate).astype(BF16)

        for h in range(2):
            hc = pl.ds(h * cw, cw)
            h1 = jnp.dot(tab[0], ub[:, hc], preferred_element_type=F32).astype(BF16)
            s1[k, :, :, hc] = h1.reshape(n, rows2, cw)
        spread(s1, r1, ss1, rs1, k)

    def stage2(k):
        arrived(r1, rs1, k)
        fcopy(k).wait()
        for h in range(2):
            hc = pl.ds(h * cw, cw)
            got = r1[k, :, :, hc].reshape(tok, cw)
            h2 = jnp.dot(tab[1], got, preferred_element_type=F32)
            f = (fv[k].astype(F32) * h2).astype(BF16)
            h3 = jnp.dot(tab[3], f, preferred_element_type=F32).astype(BF16)
            s2[k, :, :, hc] = h3.reshape(n, rows2, cw)
        spread(s2, r2, ss2, rs2, k)

    def dshalo(k, side):
        group = pl.ds(k * 3, 3)
        if side == 0:
            src, dst = dsb.at[group, pl.ds(tok, 8)], dsb.at[group, pl.ds(0, 8)]
        else:
            src, dst = dsb.at[group, pl.ds(8, 8)], dsb.at[group, pl.ds(8 + tok, 8)]
        return pltpu.make_async_remote_copy(
            src_ref=src,
            dst_ref=dst,
            send_sem=ds_s.at[k, side],
            recv_sem=ds_r.at[k, side],
            device_id={"seq": right if side == 0 else left},
            device_id_type=MESH,
        )

    def mxcopy(k):
        return pltpu.make_async_copy(ogv.at[k], mixed_hbm.at[:, cols(0, k)], mxsem.at[k])

    def stage3(k):
        arrived(r2, rs2, k)
        for h in range(2):
            got = r2[k, :, :, pl.ds(h * cw, cw)].reshape(tok, cw)
            hd[h] = jnp.dot(tab[2], got, preferred_element_type=F32)

        @pl.loop(0, tok // RT)
        def _(i):
            base = pl.multiple_of(i * RT, RT)
            at = pl.ds(base, RT)
            h4, dw = hd[0, at, :], hd[1, at, :]
            a, gate, v = (sb[k * 3 + g, at, :] for g in range(3))
            grad = ogv[k, at, :].astype(F32)
            ogv[k, at, :] = (gate * h4).astype(BF16)
            inner = pl.ds(base + 8, RT)
            dsb[k * 3, inner, :] = (dw * v).astype(BF16).astype(F32)
            dsb[k * 3 + 1, inner, :] = (grad * h4).astype(BF16).astype(F32)
            dsb[k * 3 + 2, inner, :] = (dw * a).astype(BF16).astype(F32)

        dshalo(k, 0).start()
        dshalo(k, 1).start()
        mxcopy(k).start()

    def stage4(k):
        dshalo(k, 0).wait()
        dshalo(k, 1).wait()

        @pl.when(me == 0)
        def _():
            dsb[pl.ds(k * 3, 3), pl.ds(0, 8), :] = jnp.zeros((3, 8, cw), F32)

        @pl.when(me == n - 1)
        def _():
            dsb[pl.ds(k * 3, 3), pl.ds(8 + tok, 8), :] = jnp.zeros((3, 8, cw), F32)

        def rows(i, sums):
            base = pl.multiple_of(i * RT, RT)
            out = []
            for g in range(3):
                kk = k * 3 + g
                prev, here, nxt = shifted(dsb[kk, pl.ds(base, RT + 16), :])
                t = taps[:, cols(g, k)]
                du = t[0:1] * nxt + t[1:2] * here + t[2:3] * prev
                dub[g, pl.ds(base, RT), :] = du.astype(BF16)
                for j, z in enumerate(shifted(zb[kk, pl.ds(base, RT + 16), :])):
                    out.append(
                        sums[g * 3 + j] + jnp.sum((here * z).reshape(RT // 8, 8, cw), axis=0)
                    )
            return tuple(out)

        sums = lax.fori_loop(0, tok // RT, rows, tuple(jnp.zeros((8, cw), F32) for _ in range(9)))
        sums = [jnp.sum(part, axis=0, keepdims=True) for part in sums]
        packed = jnp.concatenate(sums + [jnp.zeros((7, cw), F32)], axis=0)
        for q in range(cw // 128):
            tb[k * (cw // 128) + q] = packed[:, q * 128 : (q + 1) * 128]

        for g in range(3):
            wgb[k * 3 + g, 1 - core] = jnp.dot(
                xt[1 - core], dub[g], preferred_element_type=F32
            ).astype(BF16)
        ccopy(k).start()

        nt = (((1,), (1,)), ((), ()))

        @pl.loop(0, width // 256)
        def _(j):
            at = pl.ds(pl.multiple_of(j * 256, 256), 256)
            total = jnp.zeros((tok, 256), F32)
            for g in range(3):
                total += lax.dot_general(
                    dub[g], wv[k * 3 + g, at, :], nt, preferred_element_type=F32
                )

            @pl.when(k == 0)
            def _():
                acc[j] = total

            @pl.when(k > 0)
            def _():
                acc[j] += total

        ccopy(k).wait_recv()
        for g in range(3):
            own = jnp.dot(xt[core], dub[g], preferred_element_type=F32)
            wgb[k * 3 + g, core] = (own + cr[k * 3 + g].astype(F32)).astype(BF16)
        for d in range(1, xn):
            xcopy_out(k, lax.rem(xi + d, xn)).start()

    def ccopy(k):
        group = pl.ds(k * 3, 3)
        return pltpu.make_async_remote_copy(
            src_ref=wgb.at[group, 1 - core],
            dst_ref=cr.at[group],
            send_sem=c_s.at[k],
            recv_sem=c_r.at[k],
            device_id={"seq": sibling},
            device_id_type=MESH,
        )

    def block(q):
        return pl.ds(pl.multiple_of(q * 128, 128), 128)

    def xcopy_out(k, q):
        return pltpu.make_async_remote_copy(
            src_ref=wgb.at[pl.ds(k * 3, 3), core, block(q)],
            dst_ref=xr.at[k, xi],
            send_sem=x_s.at[k],
            recv_sem=x_r.at[k],
            device_id={"dp": q * 2 + yh},
            device_id_type=MESH,
        )

    def ycopy(k):
        return pltpu.make_async_remote_copy(
            src_ref=ys.at[k],
            dst_ref=yr.at[k],
            send_sem=y_s.at[k],
            recv_sem=y_r.at[k],
            device_id={"dp": xi * 2 + 1 - yh},
            device_id_type=MESH,
        )

    def local_wait(ref, sem):
        pltpu.make_async_copy(ref, ref, sem).wait()

    def stage5(k):
        local_wait(xr.at[k, pl.ds(0, xn - 1)], x_r.at[k])
        for g in range(3):
            total = wgb[k * 3 + g, core, block(xi), :].astype(F32)
            for d in range(1, xn):
                total += xr[k, lax.rem(xi + d, xn), g].astype(F32)
            ys[k, g] = total.astype(BF16)

        @pl.when(yh != core)
        def _():
            ycopy(k).start()

    def stage6(k):
        @pl.when(yh == core)
        def _():
            ycopy(k).wait_recv()
            for g in range(3):
                total = ys[k, g].astype(F32) + yr[k, g].astype(F32)
                fs[pl.ds((k * 3 + g) * (cw // 32), cw // 32)] = (
                    total.T.astype(BF16).reshape(cw // 32, 32, 128)
                )
            for g in range(3):

                @pl.loop(0, cw // 32)
                def _(i):
                    piece = (g * width + k * cw) // 32 + i
                    owner, slot = piece // per, lax.rem(piece, per)
                    src = fs.at[(k * 3 + g) * (cw // 32) + i]
                    dst = fr.at[me // 2, slot]

                    @pl.when(owner == me)
                    def _():
                        pltpu.make_async_copy(src, dst, f_r).start()

                    @pl.when(owner != me)
                    def _():
                        pltpu.make_async_remote_copy(
                            src_ref=src,
                            dst_ref=dst,
                            send_sem=f_s,
                            recv_sem=f_r,
                            device_id={"seq": owner},
                            device_id_type=MESH,
                        ).start()

    per = fr.shape[1]

    def taps_copy(step, src, dst, axis, peer):
        return pltpu.make_async_remote_copy(
            src_ref=src,
            dst_ref=dst,
            send_sem=t_s.at[step],
            recv_sem=t_r.at[step],
            device_id={axis: peer},
            device_id_type=MESH,
        )

    @pl.loop(0, NC)
    def _(k):
        stage1(k)

    @pl.loop(0, NC + 2)
    def _(t):
        @pl.when(t < NC)
        def _():
            stage2(t)

        @pl.when((t >= 1) & (t <= NC))
        def _():
            stage3(t - 1)

        @pl.when(t >= 2)
        def _():
            stage4(t - 2)

        @pl.when(t >= 3)
        def _():
            stage5(t - 3)

        @pl.when(t >= 4)
        def _():
            stage6(t - 4)

    tr[dpi] = tb[dpi]

    @pl.loop(1, ndp)
    def _(d):
        peer = lax.rem(dpi + d, ndp)
        taps_copy(0, tb.at[peer], tr.at[dpi], "dp", peer).start()

    igs = []
    for j in range(NC):
        fv[j] = acc[j].astype(BF16)
        copy = pltpu.make_async_copy(
            fv.at[j], ing_hbm.at[:, pl.ds(j * cw, cw)], igsem.at[j]
        )
        copy.start()
        igs.append(copy)

    stage6(NC - 2)

    local_wait(tr.at[pl.ds(0, ndp - 1)], t_r.at[0])
    total = tr[0]
    for m in range(1, ndp):
        total += tr[m]
    t2s[...] = total

    @pl.loop(1, n)
    def _(d):
        peer = lax.rem(me + d, n)
        taps_copy(1, t2s, t2r.at[me], "seq", peer).start()

    pltpu.make_async_copy(t2s, t2r.at[me], t_r.at[1]).start()
    stage5(NC - 1)
    stage6(NC - 1)

    local_wait(t2r, t_r.at[1])
    t3r[dpi] = lax.fori_loop(0, n, lambda i, c: c + t2r[i], jnp.zeros((16, 128), F32)) * factor

    @pl.loop(1, ndp)
    def _(d):
        taps_copy(2, t3r.at[dpi], t3r.at[dpi], "dp", lax.rem(dpi + d, ndp)).start()

    local_wait(fr, f_r)
    for p in range(per):
        wg_out[pl.ds(p * 32, 32), :] = (
            lax.fori_loop(
                0, n // 2, lambda i, c, p=p: c + fr[i, p].astype(F32), jnp.zeros((32, 128), F32)
            )
            * factor
        )

    local_wait(t3r.at[pl.ds(0, ndp - 1)], t_r.at[2])
    for m in range(ndp):
        for g in range(3):
            tg_out[:, pl.ds(g * width + m * 128, 128)] = t3r[m, pl.ds(g * 3, 3), :]

    @pl.loop(0, NC)
    def _(k):
        sent(s1, ss1, k)
        sent(s2, ss2, k)
        mxcopy(k).wait()
        ccopy(k).wait_send()
        local_wait(xr.at[k, pl.ds(0, xn - 1)], x_s.at[k])

        @pl.when(yh != core)
        def _():
            ycopy(k).wait_send()

    @pl.when(yh == core)
    def _():
        local_wait(fs.at[pl.ds(0, fs.shape[0] - per)], f_s)

    local_wait(tr.at[pl.ds(0, ndp - 1)], t_s.at[0])
    local_wait(t2r.at[pl.ds(0, n - 1)], t_s.at[1])
    local_wait(tr.at[pl.ds(0, ndp - 1)], t_s.at[2])
    for copy in igs:
        copy.wait()


def fused(rows, grads, w_in, taps, filt, n, ndp, factor):
    tok, width = rows.shape
    nb = tok // BLK
    cw = width // NC
    share = BLK // n
    per = 3 * width // n // 32
    assert cw == 256 and width == 128 * ndp and ndp % 2 == 0 and per * 32 * n == 3 * width
    tab = jnp.asarray(tables(n, nb))
    any_space = pl.BlockSpec(memory_space=pl.ANY)
    vmem = pl.BlockSpec(memory_space=pltpu.VMEM)
    dma = pltpu.SemaphoreType.DMA
    return pl.pallas_call(
        functools.partial(kernel, n, ndp, factor),
        out_shape=(
            jax.ShapeDtypeStruct((tok, width), BF16),
            jax.ShapeDtypeStruct((tok, width), BF16),
            jax.ShapeDtypeStruct((per * 32, 128), F32),
            jax.ShapeDtypeStruct((3, 3 * width), F32),
        ),
        in_specs=[any_space, any_space, any_space, vmem, any_space, any_space],
        out_specs=(any_space, any_space, vmem, vmem),
        scratch_shapes=[
            pltpu.VMEM((tok + 32, width), BF16),
            pltpu.VMEM((NC, tok, cw), BF16),
            pltpu.VMEM((3 * NC, width, cw), BF16),
            pltpu.VMEM((NC, tok, cw), BF16),
            pltpu.VMEM((4, tok, tok), BF16),
            pltpu.VMEM((3 * NC, tok + 16, cw), F32),
            pltpu.VMEM((3 * NC, tok, cw), F32),
            pltpu.VMEM((tok, 2 * cw), BF16),
            pltpu.VMEM((NC, n, nb * share, 2 * cw), BF16),
            pltpu.VMEM((NC, n, nb * share, 2 * cw), BF16),
            pltpu.VMEM((NC, n, nb * share, 2 * cw), BF16),
            pltpu.VMEM((NC, n, nb * share, 2 * cw), BF16),
            pltpu.VMEM((2, tok, cw), F32),
            pltpu.VMEM((3 * NC, tok + 16, cw), F32),
            pltpu.VMEM((3, tok, cw), BF16),
            pltpu.VMEM((width // 256, tok, 256), F32),
            pltpu.VMEM((2, 64 * ndp, tok), BF16),
            pltpu.VMEM((3 * NC, 2, 64 * ndp, cw), BF16),
            pltpu.VMEM((3 * NC, 64 * ndp, cw), BF16),
            pltpu.VMEM((NC, ndp // 2, 3, 128, cw), BF16),
            pltpu.VMEM((NC, 3, 128, cw), BF16),
            pltpu.VMEM((NC, 3, 128, cw), BF16),
            pltpu.VMEM((per * n, 32, 128), BF16),
            pltpu.VMEM((n // 2, per, 32, 128), BF16),
            pltpu.VMEM((ndp, 16, 128), F32),
            pltpu.VMEM((ndp, 16, 128), F32),
            pltpu.VMEM((16, 128), F32),
            pltpu.VMEM((n, 16, 128), F32),
            pltpu.VMEM((ndp, 16, 128), F32),
            dma,
            dma,
            dma((3 * NC,)),
            dma((NC,)),
            dma((NC,)),
            dma((2,)),
            dma((2,)),
            dma((NC,)),
            dma((NC,)),
            dma((NC,)),
            dma((NC,)),
            dma((NC, 2)),
            dma((NC, 2)),
            dma((NC,)),
            dma((NC,)),
            dma((NC,)),
            dma((NC,)),
            dma((NC,)),
            dma((NC,)),
            dma((NC,)),
            dma((NC,)),
            dma,
            dma,
            dma((3,)),
            dma((3,)),
        ],
        compiler_params=pltpu.CompilerParams(
            collective_id=0, has_side_effects=True, vmem_limit_bytes=67043328
        ),
        name="monarch",
    )(rows, grads, w_in, taps, filt.reshape(tok, width), tab)


def finish_kernel(mixed, ing, wg, tg, mixed_out, ing_out, wg_out, tg_out, buf, isem, osem):
    parts = isem.shape[1]
    size = mixed.shape[0] // parts

    def move(a, j, src, dst, sem):
        return pltpu.make_async_copy(src, dst, sem.at[a, j])

    def fetch(a, j):
        at = pl.ds(j * size, size)
        return move(a, j, (mixed, ing)[a].at[at], buf.at[a, at], isem)

    def put(a, j):
        at = pl.ds(j * size, size)
        return move(a, j, buf.at[a, at], (mixed_out, ing_out)[a].at[at], osem)

    pieces = [(a, j) for j in range(parts) for a in range(2)]
    for piece in pieces:
        fetch(*piece).start()
    wg_out[...] = wg[...]
    tg_out[...] = tg[...]
    for piece in pieces:
        fetch(*piece).wait()
        put(*piece).start()
    for piece in pieces:
        put(*piece).wait()


def finish(mixed, ing, wg, tg):
    any_space = pl.BlockSpec(memory_space=pl.ANY)
    vmem = pl.BlockSpec(memory_space=pltpu.VMEM)
    dma = pltpu.SemaphoreType.DMA((2, 4))
    return pl.pallas_call(
        finish_kernel,
        out_shape=(
            jax.ShapeDtypeStruct(mixed.shape, mixed.dtype),
            jax.ShapeDtypeStruct(ing.shape, ing.dtype),
            jax.ShapeDtypeStruct(wg.shape, wg.dtype),
            jax.ShapeDtypeStruct(tg.shape, tg.dtype),
        ),
        in_specs=[any_space, any_space, vmem, vmem],
        out_specs=(any_space, any_space, vmem, vmem),
        scratch_shapes=[pltpu.VMEM((2, *mixed.shape), mixed.dtype), dma, dma],
        name="finish",
    )(mixed, ing, wg, tg)


def shards(inputs, out_grad, w_in, taps, filt):
    tok = inputs.shape[1]
    nseq = lax.axis_size("seq")
    ndata = lax.axis_size("dp")
    factor = 1.0 / math.sqrt(ndata * nseq * tok)
    mixed, in_grad, w_grad, taps_grad = fused(
        inputs[0], out_grad[0], w_in, taps, filt, nseq, ndata, factor
    )
    mixed, in_grad, w_grad, taps_grad = finish(mixed, in_grad, w_grad, taps_grad)
    return (mixed[None], in_grad[None], w_grad.T, taps_grad)


def solution(mesh):
    return jax.shard_map(
        shards,
        mesh=mesh,
        in_specs=(P("dp", "seq", None), P("dp", "seq", None), P(), P(), P(None, "seq", None)),
        out_specs=(P("dp", "seq", None), P("dp", "seq", None), P("dp", "seq"), P()),
        check_vma=False,
    )
```

```python
import functools
import math

import jax
import jax.numpy as jnp
import numpy as np
from jax import lax
from jax.experimental import pallas as pl
from jax.experimental.pallas import tpu as pltpu
from jax.sharding import PartitionSpec as P

BLK = 256
NC = 4
RT = 64
MESH = pl.DeviceIdType.MESH
F32 = jnp.float32
BF16 = jnp.bfloat16


def dct_table(count):
    rows = np.arange(count, dtype=np.float32)[:, None]
    cols = np.arange(count, dtype=np.float32)[None, :]
    first = np.where(rows == 0, np.float32(math.sqrt(0.5)), np.float32(1.0))
    angle = np.float32(math.pi) * (cols + np.float32(0.5)) * rows / np.float32(count)
    table = np.float32(math.sqrt(2.0 / count)) * first * np.cos(angle.astype(np.float32))
    return table.astype(np.float32)


def tables(nseq, nb):
    share = BLK // nseq
    span = nb * nseq
    size = nb * BLK
    cq = dct_table(BLK)
    cp = dct_table(span)
    first = np.zeros((nseq, nb, share, nb, BLK), np.float32)
    for b in range(nb):
        first[:, b, :, b, :] = cq.reshape(nseq, share, BLK)
    first = first.reshape(size, size)
    second = np.zeros((span, share, span, share), np.float32)
    for r in range(share):
        second[:, r, :, r] = cp
    second = second.reshape(size, size)
    return np.stack([first, second, first.T, second.T]).astype(jnp.bfloat16)


def kernel(
    n,
    ndp,
    factor,
    x_hbm,
    og_hbm,
    w_hbm,
    taps,
    filt_hbm,
    tab_hbm,
    mixed_hbm,
    ing_hbm,
    wg_out,
    tg_out,
    xv,
    ogv,
    wv,
    fv,
    tab,
    zb,
    sb,
    ub,
    s1,
    r1,
    s2,
    r2,
    hd,
    dsb,
    dub,
    acc,
    xt,
    wgb,
    cr,
    xr,
    ys,
    yr,
    fs,
    fr,
    tb,
    tr,
    t2s,
    t2r,
    t3r,
    xsem,
    tabsem,
    wsem,
    ogsem,
    fsem,
    hs_sem,
    hr_sem,
    ss1,
    rs1,
    ss2,
    rs2,
    ds_s,
    ds_r,
    mxsem,
    igsem,
    c_s,
    c_r,
    x_s,
    x_r,
    y_s,
    y_r,
    f_s,
    f_r,
    t_s,
    t_r,
):
    tok, width = x_hbm.shape
    cw = width // NC
    rows2 = r1.shape[2]
    me = lax.axis_index("seq")
    right, left = lax.rem(me + 1, n), lax.rem(me + n - 1, n)
    dpi = lax.axis_index("dp")
    xn = ndp // 2
    xi, yh = dpi // 2, lax.rem(dpi, 2)
    core = lax.rem(me, 2)
    sibling = me + 1 - 2 * core

    def cols(g, k):
        return pl.ds(pl.multiple_of(g * width + k * cw, cw), cw)

    xcopy = pltpu.make_async_copy(x_hbm, xv.at[pl.ds(0, tok)], xsem)
    xcopy.start()

    def wcopy(k, g):
        return pltpu.make_async_copy(w_hbm.at[:, cols(g, k)], wv.at[k * 3 + g], wsem.at[k * 3 + g])

    def ogcopy(k):
        return pltpu.make_async_copy(og_hbm.at[:, cols(0, k)], ogv.at[k], ogsem.at[k])

    def fcopy(k):
        return pltpu.make_async_copy(filt_hbm.at[:, cols(0, k)], fv.at[k], fsem.at[k])

    tabcopy = pltpu.make_async_copy(tab_hbm, tab, tabsem)
    for g in range(3):
        wcopy(0, g).start()
    ogcopy(0).start()
    tabcopy.start()

    @pl.loop(1, NC)
    def _(k):
        for g in range(3):
            wcopy(k, g).start()
        ogcopy(k).start()

    @pl.loop(0, NC)
    def _(k):
        fcopy(k).start()

    barrier = pltpu.get_barrier_semaphore()

    @pl.loop(1, n)
    def _(d):
        pl.semaphore_signal(
            barrier, inc=1, device_id={"seq": lax.rem(me + d, n)}, device_id_type=MESH
        )

    @pl.loop(1, ndp)
    def _(d):
        pl.semaphore_signal(
            barrier, inc=1, device_id={"dp": lax.rem(dpi + d, ndp)}, device_id_type=MESH
        )

    xcopy.wait()
    for c in range(2):
        for q in range(xn):
            xt[c, pl.ds(q * 128, 128), :] = xv[pl.ds(0, tok), pl.ds((2 * q + c) * 128, 128)].T
    pl.semaphore_wait(barrier, n + ndp - 2)

    def xhalo(side):
        src = xv.at[pl.ds(tok - 16, 16)] if side == 0 else xv.at[pl.ds(0, 16)]
        dst = xv.at[pl.ds(tok, 16)] if side == 0 else xv.at[pl.ds(tok + 16, 16)]
        return pltpu.make_async_remote_copy(
            src_ref=src,
            dst_ref=dst,
            send_sem=hs_sem.at[side],
            recv_sem=hr_sem.at[side],
            device_id={"seq": right if side == 0 else left},
            device_id_type=MESH,
        )

    xhalo(0).start()
    xhalo(1).start()
    xhalo(0).wait()
    xhalo(1).wait()
    tabcopy.wait()
    lmask = jnp.where(me == 0, 0.0, 1.0).astype(F32)
    rmask = jnp.where(me == n - 1, 0.0, 1.0).astype(F32)

    def spread(src, dst, ssem, rsem, k):
        @pl.loop(1, n)
        def _(d):
            peer = lax.rem(me + d, n)
            pltpu.make_async_remote_copy(
                src_ref=src.at[k, peer],
                dst_ref=dst.at[k, me],
                send_sem=ssem.at[k],
                recv_sem=rsem.at[k],
                device_id={"seq": peer},
                device_id_type=MESH,
            ).start()

        pltpu.make_async_copy(src.at[k, me], dst.at[k, me], rsem.at[k]).start()

    def arrived(dst, rsem, k):
        pltpu.make_async_copy(dst.at[k], dst.at[k], rsem.at[k]).wait()

    def sent(src, ssem, k):
        part = src.at[k, pl.ds(0, n - 1)]
        pltpu.make_async_copy(part, part, ssem.at[k]).wait()

    def shifted(blk):
        size = RT + 16
        prev = pltpu.roll(blk, 1, 0)[8 : 8 + RT]
        nxt = pltpu.roll(blk, size - 1, 0)[8 : 8 + RT]
        return prev, blk[8 : 8 + RT], nxt

    def stage1(k):
        for g in range(3):
            wcopy(k, g).wait()
            kk = k * 3 + g
            z = jnp.dot(xv[...], wv[kk], preferred_element_type=F32).astype(BF16).astype(F32)
            zb[kk, pl.ds(8, tok), :] = z[:tok]
            zb[kk, pl.ds(0, 8), :] = z[tok + 8 : tok + 16] * lmask
            zb[kk, pl.ds(8 + tok, 8), :] = z[tok + 16 : tok + 24] * rmask
        ogcopy(k).wait()

        @pl.loop(0, tok // RT)
        def _(i):
            base = pl.multiple_of(i * RT, RT)
            parts = []
            for g in range(3):
                kk = k * 3 + g
                prev, here, nxt = shifted(zb[kk, pl.ds(base, RT + 16), :])
                t = taps[:, cols(g, k)]
                s = t[0:1] * prev + t[1:2] * here + t[2:3] * nxt
                sb[kk, pl.ds(base, RT), :] = s
                parts.append(s)
            a, gate, v = parts
            grad = ogv[k, pl.ds(base, RT), :].astype(F32)
            ub[pl.ds(base, RT), pl.ds(0, cw)] = (a * v).astype(BF16)
            ub[pl.ds(base, RT), pl.ds(cw, cw)] = (grad * gate).astype(BF16)

        for h in range(2):
            hc = pl.ds(h * cw, cw)
            h1 = jnp.dot(tab[0], ub[:, hc], preferred_element_type=F32).astype(BF16)
            s1[k, :, :, hc] = h1.reshape(n, rows2, cw)
        spread(s1, r1, ss1, rs1, k)

    def stage2(k):
        arrived(r1, rs1, k)
        fcopy(k).wait()
        for h in range(2):
            hc = pl.ds(h * cw, cw)
            got = r1[k, :, :, hc].reshape(tok, cw)
            h2 = jnp.dot(tab[1], got, preferred_element_type=F32)
            f = (fv[k].astype(F32) * h2).astype(BF16)
            h3 = jnp.dot(tab[3], f, preferred_element_type=F32).astype(BF16)
            s2[k, :, :, hc] = h3.reshape(n, rows2, cw)
        spread(s2, r2, ss2, rs2, k)

    def dshalo(k, side):
        group = pl.ds(k * 3, 3)
        if side == 0:
            src, dst = dsb.at[group, pl.ds(tok, 8)], dsb.at[group, pl.ds(0, 8)]
        else:
            src, dst = dsb.at[group, pl.ds(8, 8)], dsb.at[group, pl.ds(8 + tok, 8)]
        return pltpu.make_async_remote_copy(
            src_ref=src,
            dst_ref=dst,
            send_sem=ds_s.at[k, side],
            recv_sem=ds_r.at[k, side],
            device_id={"seq": right if side == 0 else left},
            device_id_type=MESH,
        )

    def mxcopy(k):
        return pltpu.make_async_copy(ogv.at[k], mixed_hbm.at[:, cols(0, k)], mxsem.at[k])

    def stage3(k):
        arrived(r2, rs2, k)
        for h in range(2):
            got = r2[k, :, :, pl.ds(h * cw, cw)].reshape(tok, cw)
            hd[h] = jnp.dot(tab[2], got, preferred_element_type=F32)

        @pl.loop(0, tok // RT)
        def _(i):
            base = pl.multiple_of(i * RT, RT)
            at = pl.ds(base, RT)
            h4, dw = hd[0, at, :], hd[1, at, :]
            a, gate, v = (sb[k * 3 + g, at, :] for g in range(3))
            grad = ogv[k, at, :].astype(F32)
            ogv[k, at, :] = (gate * h4).astype(BF16)
            inner = pl.ds(base + 8, RT)
            dsb[k * 3, inner, :] = (dw * v).astype(BF16).astype(F32)
            dsb[k * 3 + 1, inner, :] = (grad * h4).astype(BF16).astype(F32)
            dsb[k * 3 + 2, inner, :] = (dw * a).astype(BF16).astype(F32)

        dshalo(k, 0).start()
        dshalo(k, 1).start()
        mxcopy(k).start()

    def stage4(k):
        dshalo(k, 0).wait()
        dshalo(k, 1).wait()

        @pl.when(me == 0)
        def _():
            dsb[pl.ds(k * 3, 3), pl.ds(0, 8), :] = jnp.zeros((3, 8, cw), F32)

        @pl.when(me == n - 1)
        def _():
            dsb[pl.ds(k * 3, 3), pl.ds(8 + tok, 8), :] = jnp.zeros((3, 8, cw), F32)

        def rows(i, sums):
            base = pl.multiple_of(i * RT, RT)
            out = []
            for g in range(3):
                kk = k * 3 + g
                prev, here, nxt = shifted(dsb[kk, pl.ds(base, RT + 16), :])
                t = taps[:, cols(g, k)]
                du = t[0:1] * nxt + t[1:2] * here + t[2:3] * prev
                dub[g, pl.ds(base, RT), :] = du.astype(BF16)
                for j, z in enumerate(shifted(zb[kk, pl.ds(base, RT + 16), :])):
                    out.append(
                        sums[g * 3 + j] + jnp.sum((here * z).reshape(RT // 8, 8, cw), axis=0)
                    )
            return tuple(out)

        sums = lax.fori_loop(0, tok // RT, rows, tuple(jnp.zeros((8, cw), F32) for _ in range(9)))
        sums = [jnp.sum(part, axis=0, keepdims=True) for part in sums]
        packed = jnp.concatenate(sums + [jnp.zeros((7, cw), F32)], axis=0)
        for q in range(cw // 128):
            tb[k * (cw // 128) + q] = packed[:, q * 128 : (q + 1) * 128]

        for g in range(3):
            wgb[k * 3 + g, 1 - core] = jnp.dot(
                xt[1 - core], dub[g], preferred_element_type=F32
            ).astype(BF16)
        ccopy(k).start()

        nt = (((1,), (1,)), ((), ()))

        @pl.loop(0, width // 256)
        def _(j):
            at = pl.ds(pl.multiple_of(j * 256, 256), 256)
            total = jnp.zeros((tok, 256), F32)
            for g in range(3):
                total += lax.dot_general(
                    dub[g], wv[k * 3 + g, at, :], nt, preferred_element_type=F32
                )

            @pl.when(k == 0)
            def _():
                acc[j] = total

            @pl.when(k > 0)
            def _():
                acc[j] += total

        ccopy(k).wait_recv()
        for g in range(3):
            own = jnp.dot(xt[core], dub[g], preferred_element_type=F32)
            wgb[k * 3 + g, core] = (own + cr[k * 3 + g].astype(F32)).astype(BF16)
        for d in range(1, xn):
            xcopy_out(k, lax.rem(xi + d, xn)).start()

    def ccopy(k):
        group = pl.ds(k * 3, 3)
        return pltpu.make_async_remote_copy(
            src_ref=wgb.at[group, 1 - core],
            dst_ref=cr.at[group],
            send_sem=c_s.at[k],
            recv_sem=c_r.at[k],
            device_id={"seq": sibling},
            device_id_type=MESH,
        )

    def block(q):
        return pl.ds(pl.multiple_of(q * 128, 128), 128)

    def xcopy_out(k, q):
        return pltpu.make_async_remote_copy(
            src_ref=wgb.at[pl.ds(k * 3, 3), core, block(q)],
            dst_ref=xr.at[k, xi],
            send_sem=x_s.at[k],
            recv_sem=x_r.at[k],
            device_id={"dp": q * 2 + yh},
            device_id_type=MESH,
        )

    def ycopy(k):
        return pltpu.make_async_remote_copy(
            src_ref=ys.at[k],
            dst_ref=yr.at[k],
            send_sem=y_s.at[k],
            recv_sem=y_r.at[k],
            device_id={"dp": xi * 2 + 1 - yh},
            device_id_type=MESH,
        )

    def local_wait(ref, sem):
        pltpu.make_async_copy(ref, ref, sem).wait()

    def stage5(k):
        local_wait(xr.at[k, pl.ds(0, xn - 1)], x_r.at[k])
        for g in range(3):
            total = wgb[k * 3 + g, core, block(xi), :].astype(F32)
            for d in range(1, xn):
                total += xr[k, lax.rem(xi + d, xn), g].astype(F32)
            ys[k, g] = total.astype(BF16)

        @pl.when(yh != core)
        def _():
            ycopy(k).start()

    def stage6(k):
        @pl.when(yh == core)
        def _():
            ycopy(k).wait_recv()
            for g in range(3):
                total = ys[k, g].astype(F32) + yr[k, g].astype(F32)
                fs[pl.ds((k * 3 + g) * (cw // 32), cw // 32)] = (
                    total.T.astype(BF16).reshape(cw // 32, 32, 128)
                )
            for g in range(3):

                @pl.loop(0, cw // 32)
                def _(i):
                    piece = (g * width + k * cw) // 32 + i
                    owner, slot = piece // per, lax.rem(piece, per)
                    src = fs.at[(k * 3 + g) * (cw // 32) + i]
                    dst = fr.at[me // 2, slot]

                    @pl.when(owner == me)
                    def _():
                        pltpu.make_async_copy(src, dst, f_r).start()

                    @pl.when(owner != me)
                    def _():
                        pltpu.make_async_remote_copy(
                            src_ref=src,
                            dst_ref=dst,
                            send_sem=f_s,
                            recv_sem=f_r,
                            device_id={"seq": owner},
                            device_id_type=MESH,
                        ).start()

    per = fr.shape[1]

    def taps_copy(step, src, dst, axis, peer):
        return pltpu.make_async_remote_copy(
            src_ref=src,
            dst_ref=dst,
            send_sem=t_s.at[step],
            recv_sem=t_r.at[step],
            device_id={axis: peer},
            device_id_type=MESH,
        )

    @pl.loop(0, NC)
    def _(k):
        stage1(k)

    @pl.loop(0, NC + 2)
    def _(t):
        @pl.when(t < NC)
        def _():
            stage2(t)

        @pl.when(t >= 2)
        def _():
            stage4(t - 2)

        @pl.when((t >= 1) & (t <= NC))
        def _():
            stage3(t - 1)

        @pl.when(t >= 3)
        def _():
            stage5(t - 3)

        @pl.when(t >= 4)
        def _():
            stage6(t - 4)

    tr[dpi] = tb[dpi]

    @pl.loop(1, ndp)
    def _(d):
        peer = lax.rem(dpi + d, ndp)
        taps_copy(0, tb.at[peer], tr.at[dpi], "dp", peer).start()

    igs = []
    for j in range(NC):
        fv[j] = acc[j].astype(BF16)
        copy = pltpu.make_async_copy(
            fv.at[j], ing_hbm.at[:, pl.ds(j * cw, cw)], igsem.at[j]
        )
        copy.start()
        igs.append(copy)

    stage6(NC - 2)

    local_wait(tr.at[pl.ds(0, ndp - 1)], t_r.at[0])
    total = tr[0]
    for m in range(1, ndp):
        total += tr[m]
    t2s[...] = total

    @pl.loop(1, n)
    def _(d):
        peer = lax.rem(me + d, n)
        taps_copy(1, t2s, t2r.at[me], "seq", peer).start()

    pltpu.make_async_copy(t2s, t2r.at[me], t_r.at[1]).start()
    stage5(NC - 1)
    stage6(NC - 1)

    local_wait(t2r, t_r.at[1])
    t3r[dpi] = lax.fori_loop(0, n, lambda i, c: c + t2r[i], jnp.zeros((16, 128), F32)) * factor

    @pl.loop(1, ndp)
    def _(d):
        taps_copy(2, t3r.at[dpi], t3r.at[dpi], "dp", lax.rem(dpi + d, ndp)).start()

    local_wait(fr, f_r)
    for p in range(per):
        wg_out[pl.ds(p * 32, 32), :] = (
            lax.fori_loop(
                0, n // 2, lambda i, c, p=p: c + fr[i, p].astype(F32), jnp.zeros((32, 128), F32)
            )
            * factor
        )

    local_wait(t3r.at[pl.ds(0, ndp - 1)], t_r.at[2])
    for m in range(ndp):
        for g in range(3):
            tg_out[:, pl.ds(g * width + m * 128, 128)] = t3r[m, pl.ds(g * 3, 3), :]

    @pl.loop(0, NC)
    def _(k):
        sent(s1, ss1, k)
        sent(s2, ss2, k)
        mxcopy(k).wait()
        ccopy(k).wait_send()
        local_wait(xr.at[k, pl.ds(0, xn - 1)], x_s.at[k])

        @pl.when(yh != core)
        def _():
            ycopy(k).wait_send()

    @pl.when(yh == core)
    def _():
        local_wait(fs.at[pl.ds(0, fs.shape[0] - per)], f_s)

    local_wait(tr.at[pl.ds(0, ndp - 1)], t_s.at[0])
    local_wait(t2r.at[pl.ds(0, n - 1)], t_s.at[1])
    local_wait(tr.at[pl.ds(0, ndp - 1)], t_s.at[2])
    for copy in igs:
        copy.wait()


def fused(rows, grads, w_in, taps, filt, n, ndp, factor):
    tok, width = rows.shape
    nb = tok // BLK
    cw = width // NC
    share = BLK // n
    per = 3 * width // n // 32
    assert cw == 256 and width == 128 * ndp and ndp % 2 == 0 and per * 32 * n == 3 * width
    tab = jnp.asarray(tables(n, nb))
    any_space = pl.BlockSpec(memory_space=pl.ANY)
    vmem = pl.BlockSpec(memory_space=pltpu.VMEM)
    dma = pltpu.SemaphoreType.DMA
    return pl.pallas_call(
        functools.partial(kernel, n, ndp, factor),
        out_shape=(
            jax.ShapeDtypeStruct((tok, width), BF16),
            jax.ShapeDtypeStruct((tok, width), BF16),
            jax.ShapeDtypeStruct((per * 32, 128), F32),
            jax.ShapeDtypeStruct((3, 3 * width), F32),
        ),
        in_specs=[any_space, any_space, any_space, vmem, any_space, any_space],
        out_specs=(any_space, any_space, vmem, vmem),
        scratch_shapes=[
            pltpu.VMEM((tok + 32, width), BF16),
            pltpu.VMEM((NC, tok, cw), BF16),
            pltpu.VMEM((3 * NC, width, cw), BF16),
            pltpu.VMEM((NC, tok, cw), BF16),
            pltpu.VMEM((4, tok, tok), BF16),
            pltpu.VMEM((3 * NC, tok + 16, cw), F32),
            pltpu.VMEM((3 * NC, tok, cw), F32),
            pltpu.VMEM((tok, 2 * cw), BF16),
            pltpu.VMEM((NC, n, nb * share, 2 * cw), BF16),
            pltpu.VMEM((NC, n, nb * share, 2 * cw), BF16),
            pltpu.VMEM((NC, n, nb * share, 2 * cw), BF16),
            pltpu.VMEM((NC, n, nb * share, 2 * cw), BF16),
            pltpu.VMEM((2, tok, cw), F32),
            pltpu.VMEM((3 * NC, tok + 16, cw), F32),
            pltpu.VMEM((3, tok, cw), BF16),
            pltpu.VMEM((width // 256, tok, 256), F32),
            pltpu.VMEM((2, 64 * ndp, tok), BF16),
            pltpu.VMEM((3 * NC, 2, 64 * ndp, cw), BF16),
            pltpu.VMEM((3 * NC, 64 * ndp, cw), BF16),
            pltpu.VMEM((NC, ndp // 2, 3, 128, cw), BF16),
            pltpu.VMEM((NC, 3, 128, cw), BF16),
            pltpu.VMEM((NC, 3, 128, cw), BF16),
            pltpu.VMEM((per * n, 32, 128), BF16),
            pltpu.VMEM((n // 2, per, 32, 128), BF16),
            pltpu.VMEM((ndp, 16, 128), F32),
            pltpu.VMEM((ndp, 16, 128), F32),
            pltpu.VMEM((16, 128), F32),
            pltpu.VMEM((n, 16, 128), F32),
            pltpu.VMEM((ndp, 16, 128), F32),
            dma,
            dma,
            dma((3 * NC,)),
            dma((NC,)),
            dma((NC,)),
            dma((2,)),
            dma((2,)),
            dma((NC,)),
            dma((NC,)),
            dma((NC,)),
            dma((NC,)),
            dma((NC, 2)),
            dma((NC, 2)),
            dma((NC,)),
            dma((NC,)),
            dma((NC,)),
            dma((NC,)),
            dma((NC,)),
            dma((NC,)),
            dma((NC,)),
            dma((NC,)),
            dma,
            dma,
            dma((3,)),
            dma((3,)),
        ],
        compiler_params=pltpu.CompilerParams(
            collective_id=0, has_side_effects=True, vmem_limit_bytes=67043328
        ),
        name="monarch",
    )(rows, grads, w_in, taps, filt.reshape(tok, width), tab)


def finish_kernel(mixed, ing, wg, tg, mixed_out, ing_out, wg_out, tg_out, buf, isem, osem):
    parts = isem.shape[1]
    size = mixed.shape[0] // parts

    def move(a, j, src, dst, sem):
        return pltpu.make_async_copy(src, dst, sem.at[a, j])

    def fetch(a, j):
        at = pl.ds(j * size, size)
        return move(a, j, (mixed, ing)[a].at[at], buf.at[a, at], isem)

    def put(a, j):
        at = pl.ds(j * size, size)
        return move(a, j, buf.at[a, at], (mixed_out, ing_out)[a].at[at], osem)

    pieces = [(a, j) for j in range(parts) for a in range(2)]
    for piece in pieces:
        fetch(*piece).start()
    wg_out[...] = wg[...]
    tg_out[...] = tg[...]
    for piece in pieces:
        fetch(*piece).wait()
        put(*piece).start()
    for piece in pieces:
        put(*piece).wait()


def finish(mixed, ing, wg, tg):
    any_space = pl.BlockSpec(memory_space=pl.ANY)
    vmem = pl.BlockSpec(memory_space=pltpu.VMEM)
    dma = pltpu.SemaphoreType.DMA((2, 4))
    return pl.pallas_call(
        finish_kernel,
        out_shape=(
            jax.ShapeDtypeStruct(mixed.shape, mixed.dtype),
            jax.ShapeDtypeStruct(ing.shape, ing.dtype),
            jax.ShapeDtypeStruct(wg.shape, wg.dtype),
            jax.ShapeDtypeStruct(tg.shape, tg.dtype),
        ),
        in_specs=[any_space, any_space, vmem, vmem],
        out_specs=(any_space, any_space, vmem, vmem),
        scratch_shapes=[pltpu.VMEM((2, *mixed.shape), mixed.dtype), dma, dma],
        name="finish",
    )(mixed, ing, wg, tg)


def shards(inputs, out_grad, w_in, taps, filt):
    tok = inputs.shape[1]
    nseq = lax.axis_size("seq")
    ndata = lax.axis_size("dp")
    factor = 1.0 / math.sqrt(ndata * nseq * tok)
    mixed, in_grad, w_grad, taps_grad = fused(
        inputs[0], out_grad[0], w_in, taps, filt, nseq, ndata, factor
    )
    mixed, in_grad, w_grad, taps_grad = finish(mixed, in_grad, w_grad, taps_grad)
    return (mixed[None], in_grad[None], w_grad.T, taps_grad)


def solution(mesh):
    return jax.shard_map(
        shards,
        mesh=mesh,
        in_specs=(P("dp", "seq", None), P("dp", "seq", None), P(), P(), P(None, "seq", None)),
        out_specs=(P("dp", "seq", None), P("dp", "seq", None), P("dp", "seq"), P()),
        check_vma=False,
    )
```
